32 devices in a mesh: groups: 2 (over x), probe: 16 (over z, y, core).
Axes of the slice: x: 2, y: 2, z: 4, core: 2. Of those that a mesh axis runs over, the one named last changes fastest.
Arguments:
- atom_positions: float32 [2, 32768], P(None, ('groups', 'probe')), parts along dimension 1, may hold values from 0 to 512
- atom_species: int32 [32768], P(('groups', 'probe')), parts along dimension 0, may hold values from 0 to 7
- atom_slice: int32 [32768], P(('groups', 'probe')), parts along dimension 0, may hold values from 0 to 3
- species_amp: float32 [8], replicated, may hold values from 0.02 to 0.125
- species_width: float32 [8], replicated, may hold values from 2 to 8
- probe_spectrum: float32 [2, 256, 256], replicated, may hold values from -6 to 6
- window_offsets: int32 [128, 2], P(('groups', 'probe')), parts along dimension 0, may hold values from 0 to 256
- probe_shifts: int32 [128, 2], P(('groups', 'probe')), parts along dimension 0, may hold values from 0 to 255
- slice_phase: float32 [3], replicated, may hold values from 0.0002746582 to 0.001373291
Outputs:
- scan_spectrum: float32 [2, 128, 65536], P(None, 'groups', 'probe'), parts along dimension 1
The draws below stay inside these ranges and needn't reach their ends.
There are 2 independent parts, one for each index of `groups`. The reference program is written for one: setup_inputs(seed, part) draws one part's arguments, and reference() takes and returns one part's arrays. A program takes and returns all parts, laid end to end along the dimension named above; an argument that names none is the same for every part. Nothing has to cross between parts.
All inputs are finite; a program needn't handle non-finite values.
Results may differ from the reference program's by a relative error of at most 0.025.
Values may be sent and summed in bfloat16 or wider, within the bound.
No kernel may reach another device: no remote copies, remote signals or barrier semaphores. Data moves between devices by JAX's collectives and lax.ppermute only.
A program may use at most 64 MiB of HBM per device.

```python
import math
import jax
import jax.numpy as jnp
from jax import lax

G = 512
W = 256
SLICES = 4
SPECIES = 8
PROBE_DEV = 4
ATOMS = 16384
POS = 64


def with_ends(array, key, least, largest):
    place = [jax.random.randint(jax.random.fold_in(key, axis), (), 0, length) for axis, length in enumerate(array.shape)]
    main_axis = array.shape.index(max(array.shape))
    beside = place[:main_axis] + [(place[main_axis] + 1) % array.shape[main_axis]] + place[main_axis + 1:]
    return array.at[tuple(place)].set(least).at[tuple(beside)].set(largest)


def block_levels(stream_key, extent, pieces, smallest, top_value):
    gain = 1.0
    for position, parts in pieces:
        steps = jax.random.uniform(jax.random.fold_in(jax.random.fold_in(stream_key, 6), position), (parts,), jnp.float32, smallest / len(pieces), top_value / len(pieces))
        gain = gain * jnp.repeat(jnp.exp(steps), extent[position] // parts).reshape((-1,) + (1,) * (len(extent) - 1 - position))
    return gain


def normal_values(key, dims, deviation, bound, kind=jnp.bfloat16):
    array = deviation * jax.random.normal(key, dims, jnp.float32)
    return jnp.clip(array, min=-bound, max=bound).astype(kind)


def setup_inputs(seed: int = 0, part: int = 0) -> dict:
    seeds = jax.random.split(jax.random.key(seed), 10)
    own_keys = jax.random.split(jax.random.fold_in(seeds[9], part), 10)
    atom_positions = jnp.clip(512.0 * jax.random.uniform(own_keys[0], (2, ATOMS), jnp.float32) ** block_levels(own_keys[0], (2, ATOMS), ((1, 16),), -0.2, 0.2), 0.0, 512.0)
    atom_species = with_ends(jax.random.randint(own_keys[1], (ATOMS,), 0, SPECIES), jax.random.fold_in(own_keys[1], 1), 0, SPECIES - 1).astype(jnp.int32)
    atom_slice = with_ends(jax.random.randint(own_keys[2], (ATOMS,), 0, SLICES), jax.random.fold_in(own_keys[2], 1), 0, SLICES - 1).astype(jnp.int32)
    species_amp = jnp.clip(jnp.exp(jax.random.uniform(seeds[3], (SPECIES,), jnp.float32, math.log(0.02), math.log(0.125))), 0.02, 0.125)
    species_width = jnp.clip(jnp.exp(jax.random.uniform(seeds[4], (SPECIES,), jnp.float32, math.log(2.0), math.log(8.0))), 2.0, 8.0)
    probe_spectrum = normal_values(seeds[5], (2, W, W), 1.0, 6.0, jnp.float32)
    window_offsets = with_ends(jax.random.randint(own_keys[6], (POS, 2), 0, G - W + 1), jax.random.fold_in(own_keys[6], 1), 0, G - W).astype(jnp.int32)
    probe_shifts = with_ends(jax.random.randint(own_keys[7], (POS, 2), 0, W), jax.random.fold_in(own_keys[7], 1), 0, W - 1).astype(jnp.int32)
    slice_phase = jnp.clip(jnp.exp(jax.random.uniform(seeds[8], (SLICES - 1,), jnp.float32, math.log(0.0002746582), math.log(0.001373291))), 0.0002746582, 0.001373291)
    return dict(atom_positions=atom_positions, atom_species=atom_species, atom_slice=atom_slice, species_amp=species_amp, species_width=species_width, probe_spectrum=probe_spectrum, window_offsets=window_offsets, probe_shifts=probe_shifts, slice_phase=slice_phase)


def dft_tables(length):
    indices = jnp.arange(length, dtype=jnp.int32)
    angles = 2.0 * math.pi / length * (indices[:, None] * indices[None, :] % length).astype(jnp.float32)
    factor = 1.0 / math.sqrt(length)
    return ((jnp.cos(angles) * factor).astype(jnp.bfloat16), (jnp.sin(angles) * factor).astype(jnp.bfloat16))

def along_rows(real_part, imag_part, matrix, direction):
    batch_count = real_part.shape[0]
    length = real_part.shape[1]
    stacked = jnp.concatenate([real_part, imag_part], axis=0)
    product = jnp.einsum('ky,byx->bkx', matrix.astype(jnp.float32), stacked.astype(jnp.float32), precision=lax.Precision.HIGHEST)
    new_real = product[:batch_count, :length] - direction * product[batch_count:, length:]
    new_imag = product[batch_count:, :length] + direction * product[:batch_count, length:]
    return (new_real, new_imag)

def along_columns(real_part, imag_part, matrix, direction):
    batch_count = real_part.shape[0]
    length = real_part.shape[2]
    stacked = jnp.concatenate([real_part, imag_part], axis=0)
    product = jnp.einsum('byx,xl->byl', stacked.astype(jnp.float32), matrix.astype(jnp.float32), precision=lax.Precision.HIGHEST)
    new_real = product[:batch_count, :, :length] - direction * product[batch_count:, :, length:]
    new_imag = product[batch_count:, :, :length] + direction * product[:batch_count, :, length:]
    return (new_real, new_imag)

def transmit(real_part, imag_part, window):
    values = window.astype(jnp.float32)
    cosine = jnp.cos(values)
    sine = jnp.sin(values)
    return ((real_part * cosine - imag_part * sine).astype(jnp.bfloat16), (real_part * sine + imag_part * cosine).astype(jnp.bfloat16))

def frequencies(length):
    indices = jnp.arange(length, dtype=jnp.int32)
    frequency = (indices + length // 2) % length - length // 2
    squared = frequency[:, None] * frequency[:, None] + frequency[None, :] * frequency[None, :]
    aperture = (9 * squared < length * length).astype(jnp.float32)
    return (squared.astype(jnp.float32), aperture)

def multislice(probe_spectrum, shifts, windows, slice_phase):
    length = probe_spectrum.shape[-1]
    cos_table, sin_table = dft_tables(length)
    rows_matrix = jnp.concatenate([cos_table, sin_table], axis=0)
    columns_matrix = jnp.concatenate([cos_table, sin_table], axis=1)
    squared, aperture = frequencies(length)
    indices = jnp.arange(length, dtype=jnp.int32)
    phase_index = (indices[None, :, None] * shifts[:, 0][:, None, None] + indices[None, None, :] * shifts[:, 1][:, None, None]) % length
    angles = 2.0 * math.pi / length * phase_index.astype(jnp.float32)
    cosine = jnp.cos(angles)
    sine = jnp.sin(angles)
    real_part = (probe_spectrum[0] * cosine + probe_spectrum[1] * sine).astype(jnp.bfloat16)
    imag_part = (probe_spectrum[1] * cosine - probe_spectrum[0] * sine).astype(jnp.bfloat16)
    real_part, imag_part = along_rows(real_part, imag_part, rows_matrix, 1.0)
    real_part, imag_part = along_columns(real_part.astype(jnp.bfloat16), imag_part.astype(jnp.bfloat16), columns_matrix, 1.0)
    real_part, imag_part = transmit(real_part, imag_part, windows[0])
    for layer in range(len(windows) - 1):
        real_part, imag_part = along_rows(real_part, imag_part, rows_matrix, -1.0)
        real_part, imag_part = along_columns(real_part.astype(jnp.bfloat16), imag_part.astype(jnp.bfloat16), columns_matrix, -1.0)
        phases = slice_phase[layer] * squared
        prop_real = aperture * jnp.cos(phases)
        prop_imag = -aperture * jnp.sin(phases)
        new_real = (real_part * prop_real - imag_part * prop_imag).astype(jnp.bfloat16)
        new_imag = (real_part * prop_imag + imag_part * prop_real).astype(jnp.bfloat16)
        real_part, imag_part = along_rows(new_real, new_imag, rows_matrix, 1.0)
        real_part, imag_part = along_columns(real_part.astype(jnp.bfloat16), imag_part.astype(jnp.bfloat16), columns_matrix, 1.0)
        real_part, imag_part = transmit(real_part, imag_part, windows[layer + 1])
    real_part, imag_part = along_rows(real_part, imag_part, rows_matrix, -1.0)
    real_part, imag_part = along_columns(real_part.astype(jnp.bfloat16), imag_part.astype(jnp.bfloat16), columns_matrix, -1.0)
    return (aperture * (real_part * real_part + imag_part * imag_part)).astype(jnp.bfloat16)

def build_potential(atom_positions, atom_species, atom_slice, species_amp, species_width, grid, layers):
    species_ids = jnp.arange(species_amp.shape[0], dtype=jnp.int32)
    selector = (atom_species[:, None] == species_ids[None, :]).astype(jnp.float32)
    amplitude = lax.optimization_barrier(jnp.sum(selector * species_amp[None, :], axis=1))
    widths = lax.optimization_barrier(jnp.sum(selector * species_width[None, :], axis=1))
    inverse_spread = 0.5 / (widths * widths)
    pixels = jnp.arange(grid, dtype=jnp.float32)
    along_y = jnp.exp(-jnp.square(pixels[:, None] - atom_positions[0][None, :]) * inverse_spread[None, :])
    column_factor = jnp.exp(-jnp.square(pixels[None, :] - atom_positions[1][:, None]) * inverse_spread[:, None]).astype(jnp.bfloat16)

    def one_layer(layer):
        weight = amplitude * (atom_slice == layer).astype(jnp.float32)
        row_factor = (weight[None, :] * along_y).astype(jnp.bfloat16)
        return jnp.dot(row_factor, column_factor, preferred_element_type=jnp.float32).astype(jnp.bfloat16)
    return lax.map(one_layer, jnp.arange(layers, dtype=jnp.int32))

def reference(atom_positions, atom_species, atom_slice, species_amp, species_width, probe_spectrum, window_offsets, probe_shifts, slice_phase):
    potential = build_potential(atom_positions, atom_species, atom_slice, species_amp, species_width, G, SLICES)

    def block_intensity(inputs):
        corners, shifts = inputs
        crops = jax.vmap(lambda corner: lax.dynamic_slice(potential, (jnp.int32(0), corner[0], corner[1]), (SLICES, W, W)))(corners)
        windows = [crops[:, layer] for layer in range(SLICES)]
        return multislice(probe_spectrum, shifts, windows, slice_phase)
    blocks = POS // PROBE_DEV
    intensity = lax.map(block_intensity, (window_offsets.reshape(blocks, PROBE_DEV, 2), probe_shifts.reshape(blocks, PROBE_DEV, 2)))
    intensity = intensity.reshape(POS, W * W)
    cos_scan, sin_scan = dft_tables(POS)
    matrix = jnp.concatenate([cos_scan, sin_scan], axis=0)
    product = jnp.dot(matrix, intensity, preferred_element_type=jnp.float32)
    return jnp.stack([product[:POS], -product[POS:]], axis=0)
```

```python
import math

import jax
import jax.numpy as jnp
import numpy as np
from jax import lax
from jax.experimental import pallas as pl
from jax.experimental.pallas import tpu as pltpu
from jax.sharding import PartitionSpec as P

G = 512
LANES = 128
BF16 = jnp.bfloat16
F32 = jnp.float32


def cosine_fit(scale, odd):
    nodes = 0.125 * (1.0 - np.cos((np.arange(400) + 0.5) * np.pi / 400))
    f = np.sqrt(nodes)
    values = np.sin(np.pi * f) / f if odd else np.cos(np.pi * f)
    fit = np.polynomial.chebyshev.Chebyshev.fit(nodes, values, 4, domain=[0.0, 0.25])
    return [float(scale * c) for c in fit.convert(kind=np.polynomial.Polynomial).coef]


SIN_FIT = cosine_fit(2.0, True)
COS_FIT = cosine_fit(1.0, False)
TURN_HIGH = float(np.float32(np.round(2.0**16 / (2.0 * np.pi)) / 2.0**16))
TURN_LOW = float(1.0 / (2.0 * np.pi) - TURN_HIGH)


def horner(coefficients, g):
    total = coefficients[-1]
    for c in coefficients[-2::-1]:
        total = total * g + c
    return total


def cos_sin_turns(f):
    g = f * f
    twice_sine = f * horner(SIN_FIT, g)
    cosine = horner(COS_FIT, g)
    return (1.0 - 0.5 * (twice_sine * twice_sine), twice_sine * cosine)


def cos_sin(v):
    t = v * TURN_HIGH
    return cos_sin_turns((t - jnp.round(t)) + v * TURN_LOW)


def mirrored(length, tile):
    m = np.arange(length // 2).reshape(-1, tile)
    return np.concatenate([m, length - 1 - m], axis=1).reshape(-1)


def signed(half, tile):
    m = np.arange(half).reshape(-1, tile)
    k = np.concatenate([m, -m], axis=1).reshape(-1)
    second = np.concatenate([np.zeros_like(m), np.ones_like(m)], axis=1).reshape(-1) == 1
    return k, second


class Plan:
    def __init__(self, length):
        n = self.n = length
        kmax = max(k for k in range(n) if 9 * k * k < n * n)
        self.half_y = -(-(kmax + 1) // 8) * 8
        self.rows = 2 * self.half_y
        pix_y = mirrored(n, 8)
        pix_x = mirrored(n, n // 2)
        ky, second_y = signed(self.half_y, 8)
        kx, second_x = signed(n // 2, n // 2)
        scale = 1.0 / math.sqrt(n)

        def forward(freq, pix, odd_slot):
            m = np.where(odd_slot, n - 1 - pix, pix)
            angle = 2.0 * np.pi / n * np.outer(freq, m + 0.5)
            return np.where(odd_slot[None, :], np.sin(angle), np.cos(angle)) * scale

        odd_y = pix_y >= n // 2
        odd_x = pix_x >= n // 2
        self.fwd_y = forward(ky, pix_y, odd_y)
        self.fwd_x = forward(kx, pix_x, odd_x).T

        def inverse(pix, freq, second):
            angle = 2.0 * np.pi / n * np.outer(pix + 0.5, np.abs(freq))
            return np.where(second[None, :], np.sin(angle), np.cos(angle)) * scale

        self.inv_y = inverse(pix_y, ky, second_y)
        self.inv_x = inverse(pix_x, kx, second_x).T
        block = 16
        keep = -(-(kmax + 1) // block) * block
        self.keep = keep
        nat = np.concatenate([np.arange(keep), np.arange(n - keep, n)])
        self.last_y = forward(nat, pix_y, odd_y)
        self.last_x = forward(np.arange(n), pix_x, odd_x).T
        freq = (np.arange(n) + n // 2) % n - n // 2
        q2 = freq[nat][:, None] ** 2 + freq[None, :] ** 2
        self.aperture_last = (9 * q2 < n * n).astype(np.float32)
        q2 = ky[:, None] ** 2 + kx[None, :] ** 2
        self.q2 = q2.astype(np.float32)
        self.aperture = (
            (9 * q2 < n * n) & ~((ky == 0) & second_y)[:, None] & ~((kx == 0) & second_x)[None, :]
        ).astype(np.float32)
        ay = 2.0 * np.pi / n * (np.outer(pix_y, np.arange(n)) % n)
        ax = 2.0 * np.pi / n * (np.outer(np.arange(n), pix_x) % n)
        self.start_y = np.stack(
            [
                np.concatenate([np.cos(ay), -np.sin(ay)], axis=1),
                np.concatenate([np.sin(ay), np.cos(ay)], axis=1),
            ]
        ) * scale
        self.start_x = np.stack(
            [
                np.concatenate([np.cos(ax), -np.sin(ax)], axis=0),
                np.concatenate([np.sin(ax), np.cos(ax)], axis=0),
            ]
        ) * scale
        halves = G // n
        self.grid_y = np.concatenate([pix_y + n * h for h in range(halves)]).astype(np.float32)
        self.grid_x = np.concatenate([pix_x + n * h for h in range(halves)]).astype(np.float32)


def dot(a, b):
    return jnp.dot(a, b, preferred_element_type=F32)


def gather_atoms(block, devices):
    step = 2
    while step < devices:
        pairs = [(i, i ^ step) for i in range(devices)]
        block = jnp.concatenate([block, lax.ppermute(block, "probe", pairs)], axis=0)
        step *= 2
    return block


def build_body(layers, species, amp_ref, width_ref, gy_ref, gx_ref, atoms_ref, out_ref, row_ref, col_ref):
    blocks = atoms_ref.shape[1] // 3
    code = atoms_ref[0, 2 * blocks :, :]
    layer = jnp.floor(code * (1.0 / species))
    kind = code - layer * species
    amp = jnp.zeros_like(code)
    width = jnp.zeros_like(code)
    for k in range(species):
        amp = jnp.where(kind == k, amp_ref[k], amp)
        width = jnp.where(kind == k, width_ref[k], width)
    for b in range(blocks):
        lanes = slice(b * LANES, (b + 1) * LANES)
        w = width[b : b + 1, :]
        a = amp[b : b + 1, :]
        masks = [(layer[b : b + 1, :] == s).astype(F32).astype(BF16) for s in range(layers)]
        y = atoms_ref[0, b : b + 1, :]
        x = atoms_ref[0, blocks + b : blocks + b + 1, :]
        for r in range(0, G, 64):
            rows = slice(r, r + 64)
            d = gy_ref[rows, :] - y
            e = (jnp.exp2(d * d * w) * a).astype(BF16)
            for s in range(layers):
                row_ref[s, rows, lanes] = e * masks[s]
            d = gx_ref[rows, :] - x
            col_ref[rows, lanes] = jnp.exp2(d * d * w).astype(BF16)
    first = pl.program_id(0) == 0
    for s in range(layers):
        part = lax.dot_general(
            row_ref[s], col_ref[...], (((1,), (1,)), ((), ())), preferred_element_type=F32
        )

        @pl.when(first)
        def _():
            out_ref[s] = part

        @pl.when(jnp.logical_not(first))
        def _():
            out_ref[s] += part


def build(plan, atoms, amps, widths, layers):
    segments, height, lanes = atoms.shape
    species = amps.shape[0]
    atom_count = height // 3 * lanes
    grid_y = np.broadcast_to(plan.grid_y[:, None], (G, LANES))
    grid_x = np.broadcast_to(plan.grid_x[:, None], (G, LANES))
    whole = lambda *shape: pl.BlockSpec(shape, lambda i: (0,) * len(shape))
    smem = pl.BlockSpec(memory_space=pltpu.SMEM)

    def body(*refs):
        build_body(layers, species, *refs)

    return pl.pallas_call(
        body,
        out_shape=jax.ShapeDtypeStruct((layers, G, G), F32),
        grid=(segments,),
        in_specs=[
            smem,
            smem,
            whole(G, LANES),
            whole(G, LANES),
            pl.BlockSpec((1, height, lanes), lambda i: (i, 0, 0)),
        ],
        out_specs=whole(layers, G, G),
        scratch_shapes=[pltpu.VMEM((layers, G, atom_count), BF16), pltpu.VMEM((G, atom_count), BF16)],
        name="build",
    )(amps, widths, jnp.asarray(grid_y), jnp.asarray(grid_x), atoms)


def init_body(shift_ref, phase_ref, spec_ref, ty_ref, tx_ref, q2_ref, ap_ref, z_ref, prop_ref, a_ref, b_ref):
    n = spec_ref.shape[-1]
    positions = z_ref.shape[0]
    for layer in range(prop_ref.shape[0]):
        for r in range(0, q2_ref.shape[0], 16):
            rows = slice(r, r + 16)
            c, s = cos_sin(phase_ref[layer] * q2_ref[rows, :])
            prop_ref[layer, 0, rows, :] = ap_ref[rows, :] * c
            prop_ref[layer, 1, rows, :] = -(ap_ref[rows, :] * s)
    for p in range(positions):
        sy = shift_ref[p, 0]
        sx = shift_ref[p, 1]
        for r in range(0, n, 16):
            rows = slice(r, r + 16)
            ky = lax.broadcasted_iota(jnp.int32, (16, n), 0) + r
            kx = lax.broadcasted_iota(jnp.int32, (16, n), 1)
            turns = ((ky * sy + kx * sx) & (n - 1)).astype(F32) * (1.0 / n)
            c, s = cos_sin_turns(turns - jnp.round(turns))
            re = spec_ref[0, rows, :]
            im = spec_ref[1, rows, :]
            a_ref[p, rows, :] = (re * c + im * s).astype(BF16)
            a_ref[p, slice(n + r, n + r + 16), :] = (im * c - re * s).astype(BF16)
        b_ref[p, :, :n] = dot(ty_ref[0], a_ref[p]).astype(BF16)
        b_ref[p, :, n:] = dot(ty_ref[1], a_ref[p]).astype(BF16)
        z_ref[p, 0] = dot(b_ref[p], tx_ref[0])
        z_ref[p, 1] = dot(b_ref[p], tx_ref[1])


def init(plan, shifts, slice_phase, spectrum):
    n = plan.n
    positions = shifts.shape[0]
    vmem = pl.BlockSpec(memory_space=pltpu.VMEM)
    smem = pl.BlockSpec(memory_space=pltpu.SMEM)
    return pl.pallas_call(
        init_body,
        out_shape=(
            jax.ShapeDtypeStruct((positions, 2, n, n), F32),
            jax.ShapeDtypeStruct((slice_phase.shape[0], 2, plan.rows, n), F32),
        ),
        in_specs=[smem, smem, vmem, vmem, vmem, vmem, vmem],
        out_specs=(vmem, vmem),
        scratch_shapes=[pltpu.VMEM((positions, 2 * n, n), BF16), pltpu.VMEM((positions, n, 2 * n), BF16)],
        name="init",
    )(
        shifts,
        slice_phase,
        spectrum,
        jnp.asarray(plan.start_y, BF16),
        jnp.asarray(plan.start_x, BF16),
        jnp.asarray(plan.q2),
        jnp.asarray(plan.aperture),
    )


def halves(x, axis):
    h = x.shape[axis] // 2
    if axis == 0:
        return x[:h], x[h:]
    return x[:, :h], x[:, h:]


def forward_pair(re, im, axis):
    rt, rb = halves(re, axis)
    it, ib = halves(im, axis)
    u = jnp.concatenate([rt + rb, it - ib], axis=axis)
    w = jnp.concatenate([it + ib, rb - rt], axis=axis)
    return u.astype(BF16), w.astype(BF16)


def inverse_pair(re, im, axis):
    rt, rb = halves(re, axis)
    it, ib = halves(im, axis)
    u = jnp.concatenate([rt + rb, ib - it], axis=axis)
    w = jnp.concatenate([it + ib, rt - rb], axis=axis)
    return u.astype(BF16), w.astype(BF16)


def slice_body(plan, direct, off_ref, own_ref, got_ref, z0_ref, prop_ref, fy_ref, fx_ref, iy_ref, ix_ref,
               ly_ref, lx_ref, la_ref, out_ref, v_ref, z_ref, u_ref, y_ref, t_ref, x_ref, sem):
    n = plan.n
    rows_f = plan.rows
    positions = z0_ref.shape[0]
    layers = own_ref.shape[0]
    fetch = pltpu.make_async_copy(z0_ref, z_ref, sem)
    fetch.start()

    def combine(layer):
        for r in range(0, G, 16):
            rows = slice(r, r + 16)
            total = own_ref[layer, rows, :] + got_ref[layer, rows, :].astype(F32)
            v_ref[rows, :] = total.astype(BF16).astype(F32)

    lane = lax.broadcasted_iota(jnp.int32, (16, n), 1)
    pixel_x = jnp.where(lane < n // 2, lane, n + n // 2 - 1 - lane)
    sub = lax.broadcasted_iota(jnp.int32, (16, n), 0)

    def transmit(p):
        oy = off_ref[p, 0]
        ox = off_ref[p, 1]
        inside_x = pixel_x >= ox
        for g in range(n // 16):
            rows = slice(16 * g, 16 * g + 16)
            far = slice(n + 16 * g, n + 16 * g + 16)
            pixel_y = jnp.where(sub < 8, sub + 8 * g, n + 7 - 8 * g - sub)
            near_v = jnp.where(inside_x, v_ref[rows, :n], v_ref[rows, n:])
            far_v = jnp.where(inside_x, v_ref[far, :n], v_ref[far, n:])
            c, s = cos_sin(jnp.where(pixel_y >= oy, near_v, far_v))
            zr = z_ref[p, 0, rows, :]
            zi = z_ref[p, 1, rows, :]
            u, w = forward_pair(zr * c - zi * s, zr * s + zi * c, 0)
            u_ref[p, 0, rows, :] = u
            u_ref[p, 1, rows, :] = w

    def step(layer, carry):
        combine(layer)
        for p in range(positions):
            transmit(p)
            y_ref[p, 0, :rows_f] = dot(fy_ref[...], u_ref[p, 0])
            y_ref[p, 1, :rows_f] = dot(fy_ref[...], u_ref[p, 1])
            for g in range(rows_f // 16):
                rows = slice(16 * g, 16 * g + 16)
                low = slice(rows_f + 16 * g, rows_f + 16 * g + 16)
                t_ref[p, rows, :], t_ref[p, low, :] = forward_pair(y_ref[p, 0, rows, :], y_ref[p, 1, rows, :], 1)
            x_ref[p, : 2 * rows_f] = dot(t_ref[p, : 2 * rows_f], fx_ref[...])
            for g in range(rows_f // 16):
                rows = slice(16 * g, 16 * g + 16)
                low = slice(rows_f + 16 * g, rows_f + 16 * g + 16)
                re = x_ref[p, rows, :]
                im = x_ref[p, low, :]
                pr = prop_ref[layer, 0, rows, :]
                pi = prop_ref[layer, 1, rows, :]
                t_ref[p, rows, :], t_ref[p, low, :] = inverse_pair(re * pr - im * pi, re * pi + im * pr, 1)
            x_ref[p, : 2 * rows_f] = dot(t_ref[p, : 2 * rows_f], ix_ref[...])
            for g in range(rows_f // 16):
                rows = slice(16 * g, 16 * g + 16)
                low = slice(rows_f + 16 * g, rows_f + 16 * g + 16)
                t_ref[p, rows, :], t_ref[p, low, :] = inverse_pair(x_ref[p, rows, :], x_ref[p, low, :], 0)
            z_ref[p, 0] = dot(iy_ref[...], t_ref[p, :rows_f])
            z_ref[p, 1] = dot(iy_ref[...], t_ref[p, rows_f : 2 * rows_f])
        return carry

    fetch.wait()
    lax.fori_loop(0, layers - 1, step, 0)
    combine(layers - 1)
    keep = plan.keep
    for p in range(positions):
        transmit(p)
        y_ref[p, 0] = dot(ly_ref[...], u_ref[p, 0])
        y_ref[p, 1] = dot(ly_ref[...], u_ref[p, 1])
        count = 2 * keep
        for g in range(count // 16):
            rows = slice(16 * g, 16 * g + 16)
            low = slice(count + 16 * g, count + 16 * g + 16)
            t_ref[p, rows, :], t_ref[p, low, :] = forward_pair(y_ref[p, 0, rows, :], y_ref[p, 1, rows, :], 1)
        x_ref[p] = dot(t_ref[p], lx_ref[...])
        for g in range(n // 16):
            r = 16 * g
            if r < keep:
                src = r
            elif r >= n - keep:
                src = r - (n - 2 * keep)
            else:
                src = None
            if src is None:
                value = jnp.zeros((16, n), BF16)
            else:
                re = x_ref[p, slice(src, src + 16), :]
                im = x_ref[p, slice(count + src, count + src + 16), :]
                value = (la_ref[slice(src, src + 16), :] * (re * re + im * im)).astype(BF16)
            if direct:
                out_ref[g, p] = value
            else:
                out_ref[p, slice(r, r + 16), :] = value


def multislice(plan, offsets, own, got, start, prop, direct):
    n = plan.n
    positions = start.shape[0]
    vmem = pl.BlockSpec(memory_space=pltpu.VMEM)
    smem = pl.BlockSpec(memory_space=pltpu.SMEM)
    shape = (n // 16, positions, 16, n) if direct else (positions, n, n)
    count = 2 * plan.keep

    def body(*refs):
        slice_body(plan, direct, *refs)

    return pl.pallas_call(
        body,
        out_shape=jax.ShapeDtypeStruct(shape, BF16),
        in_specs=[smem, vmem, vmem, pl.BlockSpec(memory_space=pl.ANY)] + [vmem] * 8,
        out_specs=vmem,
        scratch_shapes=[
            pltpu.VMEM((G, G), F32),
            pltpu.VMEM((positions, 2, n, n), F32),
            pltpu.VMEM((positions, 2, n, n), BF16),
            pltpu.VMEM((positions, 2, count, n), F32),
            pltpu.VMEM((positions, 2 * count, n), BF16),
            pltpu.VMEM((positions, 2 * count, n), F32),
            pltpu.SemaphoreType.DMA,
        ],
        name="multislice",
    )(
        offsets,
        own,
        got,
        start,
        prop,
        jnp.asarray(plan.fwd_y, BF16),
        jnp.asarray(plan.fwd_x, BF16),
        jnp.asarray(plan.inv_y, BF16),
        jnp.asarray(plan.inv_x, BF16),
        jnp.asarray(plan.last_y, BF16),
        jnp.asarray(plan.last_x, BF16),
        jnp.asarray(plan.aperture_last),
    )


def scan_matrix(positions):
    index = np.arange(positions)
    angle = 2.0 * np.pi / positions * (np.outer(index, index) % positions)
    return np.concatenate([np.cos(angle), -np.sin(angle)]) / math.sqrt(positions)


def on_device(
    atom_positions,
    atom_species,
    atom_slice,
    species_amp,
    species_width,
    probe_spectrum,
    window_offsets,
    probe_shifts,
    slice_phase,
):
    devices = lax.axis_size("probe")
    n = probe_spectrum.shape[-1]
    layers = slice_phase.shape[0] + 1
    plan = Plan(n)
    species = species_amp.shape[0]
    atom_rows = atom_species.shape[0] // LANES
    code = (atom_slice * species + atom_species).astype(F32).reshape(atom_rows, LANES)
    atoms = jnp.concatenate([atom_positions.reshape(2 * atom_rows, LANES), code], axis=0)[None]
    widths = -0.5 * math.log2(math.e) / (species_width * species_width)
    atoms = gather_atoms(atoms, devices)
    own = build(plan, atoms, species_amp, widths, layers)
    pairs = [(i, i ^ 1) for i in range(devices)]
    got = lax.ppermute(own.astype(BF16), "probe", pairs)
    shifts = (probe_shifts + window_offsets) & (n - 1)
    start, prop = init(plan, shifts, slice_phase, probe_spectrum)
    rows = n // devices
    direct = rows % 16 == 0
    intensity = multislice(plan, window_offsets, own, got, start, prop, direct)
    positions = window_offsets.shape[0]
    if direct:
        received = lax.all_to_all(intensity, "probe", split_axis=0, concat_axis=0, tiled=True)
    else:
        pieces = intensity.reshape(positions, devices, rows, n)
        received = lax.all_to_all(pieces, "probe", split_axis=1, concat_axis=0, tiled=True)
    count = positions * devices
    received = received.reshape(count, rows * n)
    product = dot(jnp.asarray(scan_matrix(count), BF16), received)
    return product.reshape(2, count, rows * n)


def solution(mesh):
    placed = (
        P(None, ("groups", "probe")),
        P(("groups", "probe")),
        P(("groups", "probe")),
        P(),
        P(),
        P(),
        P(("groups", "probe"), None),
        P(("groups", "probe"), None),
        P(),
    )
    return jax.shard_map(
        on_device, mesh=mesh, in_specs=placed, out_specs=P(None, "groups", "probe"), check_vma=False
    )
```

```python
import math

import jax
import jax.numpy as jnp
import numpy as np
from jax import lax
from jax.experimental import pallas as pl
from jax.experimental.pallas import tpu as pltpu
from jax.sharding import PartitionSpec as P

G = 512
LANES = 128
BF16 = jnp.bfloat16
F32 = jnp.float32


def sine_fit():
    nodes = 0.125 * (1.0 - np.cos((np.arange(400) + 0.5) * np.pi / 400))
    f = np.sqrt(nodes)
    fit = np.polynomial.chebyshev.Chebyshev.fit(nodes, np.sin(np.pi * f) / f, 4, domain=[0.0, 0.25])
    return [float(c) for c in fit.convert(kind=np.polynomial.Polynomial).coef]


SIN_FIT = sine_fit()
TURN_HIGH = float(np.float32(np.round(2.0**16 / (2.0 * np.pi)) / 2.0**16))
TURN_LOW = float(1.0 / (2.0 * np.pi) - TURN_HIGH)


def horner(coefficients, g):
    total = coefficients[-1]
    for c in coefficients[-2::-1]:
        total = total * g + c
    return total


def cos_sin_turns(f):
    sine = f * horner(SIN_FIT, f * f)
    square = sine * sine
    cosine_square = jnp.maximum(1.0 - square, 1e-30)
    return (1.0 - 2.0 * square, 2.0 * sine * (cosine_square * lax.rsqrt(cosine_square)))


def cos_sin(v):
    t = v * TURN_HIGH
    return cos_sin_turns((t - jnp.round(t)) + v * TURN_LOW)


def mirrored(length, tile):
    m = np.arange(length // 2).reshape(-1, tile)
    return np.concatenate([m, length - 1 - m], axis=1).reshape(-1)


def signed(half, tile):
    m = np.arange(half).reshape(-1, tile)
    k = np.concatenate([m, -m], axis=1).reshape(-1)
    second = np.concatenate([np.zeros_like(m), np.ones_like(m)], axis=1).reshape(-1) == 1
    return k, second


class Plan:
    def __init__(self, length):
        n = self.n = length
        kmax = max(k for k in range(n) if 9 * k * k < n * n)
        self.half_y = -(-(kmax + 1) // 8) * 8
        self.rows = 2 * self.half_y
        pix_y = mirrored(n, 8)
        pix_x = mirrored(n, n // 2)
        ky, second_y = signed(self.half_y, 8)
        kx, second_x = signed(n // 2, n // 2)
        scale = 1.0 / math.sqrt(n)

        def forward(freq, pix, odd_slot):
            m = np.where(odd_slot, n - 1 - pix, pix)
            angle = 2.0 * np.pi / n * np.outer(freq, m + 0.5)
            return np.where(odd_slot[None, :], np.sin(angle), np.cos(angle)) * scale

        odd_y = pix_y >= n // 2
        odd_x = pix_x >= n // 2
        self.fwd_y = forward(ky, pix_y, odd_y)
        self.fwd_x = forward(kx, pix_x, odd_x).T

        def inverse(pix, freq, second):
            angle = 2.0 * np.pi / n * np.outer(pix + 0.5, np.abs(freq))
            return np.where(second[None, :], np.sin(angle), np.cos(angle)) * scale

        self.inv_y = inverse(pix_y, ky, second_y)
        self.inv_x = inverse(pix_x, kx, second_x).T
        block = 16
        keep = -(-(kmax + 1) // block) * block
        self.keep = keep
        nat = np.concatenate([np.arange(keep), np.arange(n - keep, n)])
        self.last_y = forward(nat, pix_y, odd_y)
        self.last_x = forward(np.arange(n), pix_x, odd_x).T
        freq = (np.arange(n) + n // 2) % n - n // 2
        q2 = freq[nat][:, None] ** 2 + freq[None, :] ** 2
        self.aperture_last = (9 * q2 < n * n).astype(np.float32)
        q2 = ky[:, None] ** 2 + kx[None, :] ** 2
        self.q2 = q2.astype(np.float32)
        self.aperture = (
            (9 * q2 < n * n) & ~((ky == 0) & second_y)[:, None] & ~((kx == 0) & second_x)[None, :]
        ).astype(np.float32)
        ay = 2.0 * np.pi / n * (np.outer(pix_y, np.arange(n)) % n)
        ax = 2.0 * np.pi / n * (np.outer(np.arange(n), pix_x) % n)
        self.start_y = np.stack(
            [
                np.concatenate([np.cos(ay), -np.sin(ay)], axis=1),
                np.concatenate([np.sin(ay), np.cos(ay)], axis=1),
            ]
        ) * scale
        self.start_x = np.stack(
            [
                np.concatenate([np.cos(ax), -np.sin(ax)], axis=0),
                np.concatenate([np.sin(ax), np.cos(ax)], axis=0),
            ]
        ) * scale


def dot(a, b):
    return jnp.dot(a, b, preferred_element_type=F32)


def gather_atoms(block, devices):
    steps = []
    step = 2
    while step < devices:
        steps.append(step)
        step *= 2
    for step in steps[:-1]:
        block = jnp.concatenate([block, swap(block, step, devices)], axis=0)
    if not steps:
        return [block]
    return [block, swap(block, steps[-1], devices)]


def swap(block, step, devices):
    return lax.ppermute(block, "probe", [(i, i ^ step) for i in range(devices)])


def sort_body(layers, species, pos_ref, kind_ref, layer_ref, kind_row_ref, layer_row_ref, out_ref, one_ref):
    rows = layer_ref.shape[0]
    count = rows * LANES
    owned = [(layer_ref[...] == s).astype(F32) for s in range(layers)]
    onehot = jnp.concatenate(owned, axis=0).astype(BF16)
    i = lax.broadcasted_iota(jnp.int32, (LANES, LANES), 0)
    j = lax.broadcasted_iota(jnp.int32, (LANES, LANES), 1)
    rank = dot(onehot, (i < j).astype(F32).astype(BF16))
    total = dot(onehot, jnp.ones((LANES, LANES), BF16)).astype(BF16)
    height = layers * rows
    i = lax.broadcasted_iota(jnp.int32, (height, height), 0)
    j = lax.broadcasted_iota(jnp.int32, (height, height), 1)
    rank = rank + dot((j < i).astype(F32).astype(BF16), total)
    place = jnp.zeros((rows, LANES), F32)
    for s in range(layers):
        place = place + owned[s] * rank[s * rows : (s + 1) * rows, :]
    place = place.astype(jnp.int32)
    sub = lax.broadcasted_iota(jnp.int32, (16, 2 * LANES), 0)
    for b in range(0, rows, 2):
        wanted = jnp.concatenate([place[b : b + 1, :], place[b + 1 : b + 2, :]], axis=1)
        for r in range(0, count, 16):
            hit = (sub + r == wanted).astype(F32).astype(BF16)
            one_ref[slice(r, r + 16), slice(b * LANES, (b + 2) * LANES)] = hit
    code = (kind_row_ref[...] + species * layer_row_ref[...]).astype(F32)
    values = jnp.concatenate([pos_ref[...], code], axis=0)
    high = values.astype(BF16)
    rest = values - high.astype(F32)
    middle = rest.astype(BF16)
    low = (rest - middle.astype(F32)).astype(BF16)
    parts = [
        lax.dot_general(p, one_ref[...], (((1,), (1,)), ((), ())), preferred_element_type=F32)
        for p in (high, middle, low)
    ]
    out_ref[0] = (parts[0] + parts[1]) + parts[2]


def sort_atoms(positions, kind, layer, layers, species):
    count = kind.shape[0]
    rows = count // LANES

    def body(*refs):
        sort_body(layers, species, *refs)

    return pl.pallas_call(
        body,
        out_shape=jax.ShapeDtypeStruct((1, 3, count), F32),
        scratch_shapes=[pltpu.VMEM((count, count), BF16)],
        name="sort",
    )(
        positions,
        kind.reshape(rows, LANES),
        layer.reshape(rows, LANES),
        kind.reshape(1, count),
        layer.reshape(1, count),
    )


def build_body(layers, species, n, amp_ref, width_ref, *refs):
    *atom_refs, out_ref, gy_ref, gx_ref, acc_ref, all_ref, bound_ref, row_a, col_a, lay_a, row_b, col_b, lay_b = refs
    count = all_ref.shape[-1]
    chunks = count // LANES
    window = min(4, chunks)
    sub = lax.broadcasted_iota(jnp.int32, (16, LANES), 0)
    for h in range(G // n):
        for r in range(0, n, 16):
            rows = slice(h * n + r, h * n + r + 16)
            pixel = jnp.where(sub < 8, sub + r // 2, n + 7 - r // 2 - sub) + h * n
            gy_ref[rows, :] = pixel.astype(F32)
            pixel = jnp.where(sub + r < n // 2, sub + r, n + n // 2 - 1 - r - sub) + h * n
            gx_ref[rows, :] = pixel.astype(F32)
    filled = 0
    for ref in atom_refs:
        all_ref[filled : filled + ref.shape[0]] = ref[...]
        filled += ref.shape[0]

    segments = filled

    def find_bounds(segment, carry):
        layer = jnp.floor(all_ref[segment, 2:3, :] * (1.0 / species))
        bound_ref[segment, 0] = 0
        for s in range(1, layers):
            bound_ref[segment, s] = jnp.sum((layer < s).astype(F32)).astype(jnp.int32)
        bound_ref[segment, layers] = count
        return carry

    lax.fori_loop(0, segments, find_bounds, 0, unroll=min(segments, 8))

    def factors(segment, b, row_ref, col_ref, lay_ref):
        static = isinstance(b, int)
        lanes = slice(b * LANES, (b + 1) * LANES) if static else pl.ds(pl.multiple_of(b * LANES, LANES), LANES)
        code = all_ref[segment, 2:3, lanes]
        layer = jnp.floor(code * (1.0 / species))
        kind = code - layer * species
        a = jnp.zeros_like(code)
        w = jnp.ones_like(code)
        for k in range(species):
            a = jnp.where(kind == k, amp_ref[k], a)
            w = jnp.where(kind == k, width_ref[k], w)
        w = (-0.5 * math.log2(math.e)) / (w * w)
        lay_ref[b] = layer
        y = all_ref[segment, 0:1, lanes]
        x = all_ref[segment, 1:2, lanes]
        for r in range(0, G, 16):
            rows = slice(r, r + 16)
            d = gy_ref[rows, :] - y
            row_ref[b, rows, :] = (jnp.exp2(d * d * w) * a).astype(BF16)
            d = gx_ref[rows, :] - x
            col_ref[b, rows, :] = jnp.exp2(d * d * w).astype(BF16)

    def add_window(s, low, row_ref, col_ref, lay_ref):
        at = jnp.minimum(low, chunks - window)
        rows = []
        columns = []
        for k in range(window):
            mask = (lay_ref[at + k] == s) & (at + k >= low)
            rows.append(row_ref[at + k])
            columns.append(col_ref[at + k] * mask.astype(F32).astype(BF16))
        acc_ref[s] += lax.dot_general(
            jnp.concatenate(rows, axis=1),
            jnp.concatenate(columns, axis=1),
            (((1,), (1,)), ((), ())),
            preferred_element_type=F32,
        )

    acc_ref[...] = jnp.zeros_like(acc_ref)
    a_refs = (row_a, col_a, lay_a)
    b_refs = (row_b, col_b, lay_b)
    share = -(-chunks // layers)

    def low_of(segment, s):
        return bound_ref[segment, s] // LANES

    def all_factors(segment, refs):
        def one(b, carry):
            factors(segment, b, *refs)
            return carry

        lax.fori_loop(0, chunks, one, 0)

    def overlap(segment, refs, following, next_refs, over):
        for s in range(layers):
            low = low_of(segment, s)
            add_window(s, low, *refs)
            for b in range(s * share, min((s + 1) * share, chunks)):
                factors(following, b, *next_refs)
            over = jnp.maximum(over, bound_ref[segment, s + 1] - (low + window) * LANES)
        return over

    all_factors(0, a_refs)
    over = jnp.int32(0)
    last = segments - 1

    def pair(i, over):
        over = overlap(2 * i, a_refs, jnp.minimum(2 * i + 1, last), b_refs, over)
        return overlap(2 * i + 1, b_refs, jnp.minimum(2 * i + 2, last), a_refs, over)

    if segments > 1:
        over = lax.fori_loop(0, segments // 2, pair, over)
    else:
        over = overlap(0, a_refs, 0, b_refs, over)

    @pl.when(over > 0)
    def _():
        def segment_rest(segment, carry):
            all_factors(segment, a_refs)

            def slice_rest(s, carry):
                low = low_of(segment, s)
                chunk_end = (bound_ref[segment, s + 1] + LANES - 1) // LANES

                def more(t, carry):
                    add_window(s, low + t * window, *a_refs)
                    return carry

                return lax.fori_loop(1, (chunk_end - low + window - 1) // window, more, carry)

            return lax.fori_loop(0, layers, slice_rest, carry)

        lax.fori_loop(0, segments, segment_rest, 0)

    for s in range(layers):
        for r in range(0, G, 16):
            rows = slice(r, r + 16)
            out_ref[s, rows, :] = acc_ref[s, rows, :].astype(BF16)


def build(plan, atoms, amps, widths, layers):
    species = amps.shape[0]
    count = atoms[0].shape[-1]
    vmem = pl.BlockSpec(memory_space=pltpu.VMEM)
    smem = pl.BlockSpec(memory_space=pltpu.SMEM)

    def body(*refs):
        build_body(layers, species, plan.n, *refs)

    blocks = (count // LANES, G, LANES)
    buffers = [pltpu.VMEM(blocks, BF16), pltpu.VMEM(blocks, BF16), pltpu.VMEM((count // LANES, 1, LANES), F32)]
    return pl.pallas_call(
        body,
        out_shape=jax.ShapeDtypeStruct((layers, G, G), BF16),
        in_specs=[smem, smem] + [vmem] * len(atoms),
        out_specs=vmem,
        scratch_shapes=[
            pltpu.VMEM((G, LANES), F32),
            pltpu.VMEM((G, LANES), F32),
            pltpu.VMEM((layers, G, G), F32),
            pltpu.VMEM((sum(a.shape[0] for a in atoms), 3, count), F32),
            pltpu.SMEM((sum(a.shape[0] for a in atoms), layers + 1), jnp.int32),
        ]
        + buffers
        + buffers,
        name="build",
    )(amps, widths, *atoms)


def init_body(with_prop, *refs):
    if with_prop:
        shift_ref, phase_ref, spec_ref, ty_ref, tx_ref, q2_ref, ap_ref, z_ref, prop_ref, a_ref, b_ref = refs
        for layer in range(prop_ref.shape[0]):
            for r in range(0, q2_ref.shape[0], 16):
                rows = slice(r, r + 16)
                c, s = cos_sin(phase_ref[layer] * q2_ref[rows, :])
                prop_ref[layer, 0, rows, :] = ap_ref[rows, :] * c
                prop_ref[layer, 1, rows, :] = -(ap_ref[rows, :] * s)
    else:
        shift_ref, spec_ref, ty_ref, tx_ref, z_ref, a_ref, b_ref = refs
    n = spec_ref.shape[-1]
    positions = z_ref.shape[0]
    for p in range(positions):
        sy = shift_ref[p, 0]
        sx = shift_ref[p, 1]
        for r in range(0, n, 16):
            rows = slice(r, r + 16)
            ky = lax.broadcasted_iota(jnp.int32, (16, n), 0) + r
            kx = lax.broadcasted_iota(jnp.int32, (16, n), 1)
            turns = ((ky * sy + kx * sx) & (n - 1)).astype(F32) * (1.0 / n)
            c, s = cos_sin_turns(turns - jnp.round(turns))
            re = spec_ref[0, rows, :]
            im = spec_ref[1, rows, :]
            a_ref[p, rows, :] = (re * c + im * s).astype(BF16)
            a_ref[p, slice(n + r, n + r + 16), :] = (im * c - re * s).astype(BF16)
        b_ref[p, :, :n] = dot(ty_ref[0], a_ref[p]).astype(BF16)
        b_ref[p, :, n:] = dot(ty_ref[1], a_ref[p]).astype(BF16)
        z_ref[p, 0] = dot(b_ref[p], tx_ref[0])
        z_ref[p, 1] = dot(b_ref[p], tx_ref[1])


def init(plan, shifts, slice_phase, spectrum):
    n = plan.n
    positions = shifts.shape[0]
    vmem = pl.BlockSpec(memory_space=pltpu.VMEM)
    smem = pl.BlockSpec(memory_space=pltpu.SMEM)
    with_prop = slice_phase is not None
    tables = (jnp.asarray(plan.start_y, BF16), jnp.asarray(plan.start_x, BF16))
    waves = jax.ShapeDtypeStruct((positions, 2, n, n), F32)
    if with_prop:
        args = (shifts, slice_phase, spectrum, *tables, jnp.asarray(plan.q2), jnp.asarray(plan.aperture))
        specs = [smem, smem, vmem, vmem, vmem, vmem, vmem]
        out = (waves, jax.ShapeDtypeStruct((slice_phase.shape[0], 2, plan.rows, n), F32))
    else:
        args = (shifts, spectrum, *tables)
        specs = [smem, vmem, vmem, vmem]
        out = waves

    def body(*refs):
        init_body(with_prop, *refs)

    return pl.pallas_call(
        body,
        out_shape=out,
        in_specs=specs,
        out_specs=(vmem, vmem) if with_prop else vmem,
        scratch_shapes=[pltpu.VMEM((positions, 2 * n, n), BF16), pltpu.VMEM((positions, n, 2 * n), BF16)],
        name="init",
    )(*args)


def halves(x, axis):
    h = x.shape[axis] // 2
    if axis == 0:
        return x[:h], x[h:]
    return x[:, :h], x[:, h:]


def forward_pair(re, im, axis):
    rt, rb = halves(re, axis)
    it, ib = halves(im, axis)
    u = jnp.concatenate([rt + rb, it - ib], axis=axis)
    w = jnp.concatenate([it + ib, rb - rt], axis=axis)
    return u.astype(BF16), w.astype(BF16)


def inverse_pair(re, im, axis):
    rt, rb = halves(re, axis)
    it, ib = halves(im, axis)
    u = jnp.concatenate([rt + rb, ib - it], axis=axis)
    w = jnp.concatenate([it + ib, rt - rb], axis=axis)
    return u.astype(BF16), w.astype(BF16)


def slice_body(plan, direct, off_ref, own_ref, got_ref, za_ref, zb_ref, prop_ref, fy_ref, fx_ref, iy_ref, ix_ref,
               ly_ref, lx_ref, la_ref, out_ref, part_ref, v_ref, z_ref, u_ref, y_ref, t_ref, x_ref, sem, wave_sem):
    n = plan.n
    rows_f = plan.rows
    half = za_ref.shape[0]
    positions = half + zb_ref.shape[0]
    layers = own_ref.shape[0]

    def fetch(layer):
        return [
            pltpu.make_async_copy(own_ref.at[layer], part_ref.at[0, layer], sem.at[0, layer]),
            pltpu.make_async_copy(got_ref.at[layer], part_ref.at[1, layer], sem.at[1, layer]),
        ]

    waves = [
        pltpu.make_async_copy(za_ref, z_ref.at[:half], wave_sem.at[0]),
        pltpu.make_async_copy(zb_ref, z_ref.at[half:], wave_sem.at[1]),
    ]
    for copy in fetch(0):
        copy.start()
    for copy in waves:
        copy.start()
    for layer in range(1, layers):
        for copy in fetch(layer):
            copy.start()

    def combine(layer):
        for copy in fetch(layer):
            copy.wait()
        for r in range(0, G, 16):
            rows = slice(r, r + 16)
            total = part_ref[0, layer, rows, :].astype(F32) + part_ref[1, layer, rows, :].astype(F32)
            v_ref[rows, :] = total.astype(BF16).astype(F32)

    lane = lax.broadcasted_iota(jnp.int32, (16, n), 1)
    pixel_x = jnp.where(lane < n // 2, lane, n + n // 2 - 1 - lane)
    sub = lax.broadcasted_iota(jnp.int32, (16, n), 0)

    def transmit(p):
        oy = off_ref[p, 0]
        ox = off_ref[p, 1]
        inside_x = pixel_x >= ox
        for g in range(n // 16):
            rows = slice(16 * g, 16 * g + 16)
            far = slice(n + 16 * g, n + 16 * g + 16)
            pixel_y = jnp.where(sub < 8, sub + 8 * g, n + 7 - 8 * g - sub)
            near_v = jnp.where(inside_x, v_ref[rows, :n], v_ref[rows, n:])
            far_v = jnp.where(inside_x, v_ref[far, :n], v_ref[far, n:])
            c, s = cos_sin(jnp.where(pixel_y >= oy, near_v, far_v))
            zr = z_ref[p, 0, rows, :]
            zi = z_ref[p, 1, rows, :]
            u, w = forward_pair(zr * c - zi * s, zr * s + zi * c, 0)
            u_ref[p, 0, rows, :] = u
            u_ref[p, 1, rows, :] = w

    def step(layer, carry):
        combine(layer)
        for p in range(positions):
            transmit(p)
            y_ref[p, 0, :rows_f] = dot(fy_ref[...], u_ref[p, 0])
            y_ref[p, 1, :rows_f] = dot(fy_ref[...], u_ref[p, 1])
            for g in range(rows_f // 16):
                rows = slice(16 * g, 16 * g + 16)
                low = slice(rows_f + 16 * g, rows_f + 16 * g + 16)
                t_ref[p, rows, :], t_ref[p, low, :] = forward_pair(y_ref[p, 0, rows, :], y_ref[p, 1, rows, :], 1)
            x_ref[p, : 2 * rows_f] = dot(t_ref[p, : 2 * rows_f], fx_ref[...])
            for g in range(rows_f // 16):
                rows = slice(16 * g, 16 * g + 16)
                low = slice(rows_f + 16 * g, rows_f + 16 * g + 16)
                re = x_ref[p, rows, :]
                im = x_ref[p, low, :]
                pr = prop_ref[layer, 0, rows, :]
                pi = prop_ref[layer, 1, rows, :]
                t_ref[p, rows, :], t_ref[p, low, :] = inverse_pair(re * pr - im * pi, re * pi + im * pr, 1)
            x_ref[p, : 2 * rows_f] = dot(t_ref[p, : 2 * rows_f], ix_ref[...])
            for g in range(rows_f // 16):
                rows = slice(16 * g, 16 * g + 16)
                low = slice(rows_f + 16 * g, rows_f + 16 * g + 16)
                t_ref[p, rows, :], t_ref[p, low, :] = inverse_pair(x_ref[p, rows, :], x_ref[p, low, :], 0)
            z_ref[p, 0] = dot(iy_ref[...], t_ref[p, :rows_f])
            z_ref[p, 1] = dot(iy_ref[...], t_ref[p, rows_f : 2 * rows_f])
        return carry

    for copy in waves:
        copy.wait()
    lax.fori_loop(0, layers - 1, step, 0)
    combine(layers - 1)
    keep = plan.keep
    for p in range(positions):
        transmit(p)
        y_ref[p, 0] = dot(ly_ref[...], u_ref[p, 0])
        y_ref[p, 1] = dot(ly_ref[...], u_ref[p, 1])
        count = 2 * keep
        for g in range(count // 16):
            rows = slice(16 * g, 16 * g + 16)
            low = slice(count + 16 * g, count + 16 * g + 16)
            t_ref[p, rows, :], t_ref[p, low, :] = forward_pair(y_ref[p, 0, rows, :], y_ref[p, 1, rows, :], 1)
        x_ref[p] = dot(t_ref[p], lx_ref[...])
        for g in range(n // 16):
            r = 16 * g
            if r < keep:
                src = r
            elif r >= n - keep:
                src = r - (n - 2 * keep)
            else:
                src = None
            if src is None:
                value = jnp.zeros((16, n), BF16)
            else:
                re = x_ref[p, slice(src, src + 16), :]
                im = x_ref[p, slice(count + src, count + src + 16), :]
                value = (la_ref[slice(src, src + 16), :] * (re * re + im * im)).astype(BF16)
            if direct:
                out_ref[g, p] = value
            else:
                out_ref[p, slice(r, r + 16), :] = value


def multislice(plan, offsets, own, got, start, prop, direct):
    n = plan.n
    positions = offsets.shape[0]
    vmem = pl.BlockSpec(memory_space=pltpu.VMEM)
    smem = pl.BlockSpec(memory_space=pltpu.SMEM)
    anywhere = pl.BlockSpec(memory_space=pl.ANY)
    shape = (n // 16, positions, 16, n) if direct else (positions, n, n)
    count = 2 * plan.keep

    def body(*refs):
        slice_body(plan, direct, *refs)

    return pl.pallas_call(
        body,
        out_shape=jax.ShapeDtypeStruct(shape, BF16),
        in_specs=[smem] + [anywhere] * 4 + [vmem] * 8,
        out_specs=vmem,
        scratch_shapes=[
            pltpu.VMEM((2,) + own.shape, BF16),
            pltpu.VMEM((G, G), F32),
            pltpu.VMEM((positions, 2, n, n), F32),
            pltpu.VMEM((positions, 2, n, n), BF16),
            pltpu.VMEM((positions, 2, count, n), F32),
            pltpu.VMEM((positions, 2 * count, n), BF16),
            pltpu.VMEM((positions, 2 * count, n), F32),
            pltpu.SemaphoreType.DMA((2, own.shape[0])),
            pltpu.SemaphoreType.DMA((2,)),
        ],
        name="multislice",
    )(
        offsets,
        own,
        got,
        *start,
        prop,
        jnp.asarray(plan.fwd_y, BF16),
        jnp.asarray(plan.fwd_x, BF16),
        jnp.asarray(plan.inv_y, BF16),
        jnp.asarray(plan.inv_x, BF16),
        jnp.asarray(plan.last_y, BF16),
        jnp.asarray(plan.last_x, BF16),
        jnp.asarray(plan.aperture_last),
    )


def scan_matrix(positions):
    index = np.arange(positions)
    angle = 2.0 * np.pi / positions * (np.outer(index, index) % positions)
    return np.concatenate([np.cos(angle), -np.sin(angle)]) / math.sqrt(positions)


def on_device(
    atom_positions,
    atom_species,
    atom_slice,
    species_amp,
    species_width,
    probe_spectrum,
    window_offsets,
    probe_shifts,
    slice_phase,
):
    devices = lax.axis_size("probe")
    n = probe_spectrum.shape[-1]
    layers = slice_phase.shape[0] + 1
    plan = Plan(n)
    species = species_amp.shape[0]
    atoms = sort_atoms(atom_positions, atom_species, atom_slice, layers, species)
    atoms = gather_atoms(atoms, devices)
    shifts = (probe_shifts + window_offsets) & (n - 1)
    half = shifts.shape[0] // 2
    start_a, prop = init(plan, shifts[:half], slice_phase, probe_spectrum)
    *atoms, start_a, prop = lax.optimization_barrier((*atoms, start_a, prop))
    own = build(plan, atoms, species_amp, species_width, layers)
    got = swap(own, 1, devices)
    shifts, own = lax.optimization_barrier((shifts[half:], own))
    start_b = init(plan, shifts, None, probe_spectrum)
    rows = n // devices
    direct = rows % 16 == 0
    intensity = multislice(plan, window_offsets, own, got, (start_a, start_b), prop, direct)
    positions = window_offsets.shape[0]
    if direct:
        received = lax.all_to_all(intensity, "probe", split_axis=0, concat_axis=0, tiled=True)
    else:
        pieces = intensity.reshape(positions, devices, rows, n)
        received = lax.all_to_all(pieces, "probe", split_axis=1, concat_axis=0, tiled=True)
    count = positions * devices
    received = received.reshape(count, rows * n)
    product = dot(jnp.asarray(scan_matrix(count), BF16), received)
    return product.reshape(2, count, rows * n)


def solution(mesh):
    placed = (
        P(None, ("groups", "probe")),
        P(("groups", "probe")),
        P(("groups", "probe")),
        P(),
        P(),
        P(),
        P(("groups", "probe"), None),
        P(("groups", "probe"), None),
        P(),
    )
    return jax.shard_map(
        on_device, mesh=mesh, in_specs=placed, out_specs=P(None, "groups", "probe"), check_vma=False
    )
```

```python
import math

import jax
import jax.numpy as jnp
import numpy as np
from jax import lax
from jax.experimental import pallas as pl
from jax.experimental.pallas import tpu as pltpu
from jax.sharding import PartitionSpec as P

G = 512
LANES = 128
BF16 = jnp.bfloat16
F32 = jnp.float32


def sine_fit():
    nodes = 0.125 * (1.0 - np.cos((np.arange(400) + 0.5) * np.pi / 400))
    f = np.sqrt(nodes)
    fit = np.polynomial.chebyshev.Chebyshev.fit(nodes, np.sin(np.pi * f) / f, 4, domain=[0.0, 0.25])
    return [float(c) for c in fit.convert(kind=np.polynomial.Polynomial).coef]


SIN_FIT = sine_fit()
TURN_HIGH = float(np.float32(np.round(2.0**16 / (2.0 * np.pi)) / 2.0**16))
TURN_LOW = float(1.0 / (2.0 * np.pi) - TURN_HIGH)


def horner(coefficients, g):
    total = coefficients[-1]
    for c in coefficients[-2::-1]:
        total = total * g + c
    return total


def cos_sin_turns(f):
    sine = f * horner(SIN_FIT, f * f)
    square = sine * sine
    cosine_square = jnp.maximum(1.0 - square, 1e-30)
    return (1.0 - 2.0 * square, 2.0 * sine * (cosine_square * lax.rsqrt(cosine_square)))


def cos_sin(v):
    t = v * TURN_HIGH
    return cos_sin_turns((t - jnp.round(t)) + v * TURN_LOW)


def mirrored(length, tile):
    m = np.arange(length // 2).reshape(-1, tile)
    return np.concatenate([m, length - 1 - m], axis=1).reshape(-1)


def signed(half, tile):
    m = np.arange(half).reshape(-1, tile)
    k = np.concatenate([m, -m], axis=1).reshape(-1)
    second = np.concatenate([np.zeros_like(m), np.ones_like(m)], axis=1).reshape(-1) == 1
    return k, second


class Plan:
    def __init__(self, length):
        n = self.n = length
        kmax = max(k for k in range(n) if 9 * k * k < n * n)
        self.half_y = -(-(kmax + 1) // 8) * 8
        self.rows = 2 * self.half_y
        pix_y = mirrored(n, 8)
        pix_x = mirrored(n, n // 2)
        ky, second_y = signed(self.half_y, 8)
        kx, second_x = signed(n // 2, n // 2)
        scale = 1.0 / math.sqrt(n)

        def forward(freq, pix, odd_slot):
            m = np.where(odd_slot, n - 1 - pix, pix)
            angle = 2.0 * np.pi / n * np.outer(freq, m + 0.5)
            return np.where(odd_slot[None, :], np.sin(angle), np.cos(angle)) * scale

        odd_y = pix_y >= n // 2
        odd_x = pix_x >= n // 2
        self.fwd_y = forward(ky, pix_y, odd_y)
        self.fwd_x = forward(kx, pix_x, odd_x).T

        def inverse(pix, freq, second):
            angle = 2.0 * np.pi / n * np.outer(pix + 0.5, np.abs(freq))
            return np.where(second[None, :], np.sin(angle), np.cos(angle)) * scale

        self.inv_y = inverse(pix_y, ky, second_y)
        self.inv_x = inverse(pix_x, kx, second_x).T
        block = 16
        keep = -(-(kmax + 1) // block) * block
        self.keep = keep
        nat = np.concatenate([np.arange(keep), np.arange(n - keep, n)])
        self.last_y = forward(nat, pix_y, odd_y)
        self.last_x = forward(np.arange(n), pix_x, odd_x).T
        freq = (np.arange(n) + n // 2) % n - n // 2
        q2 = freq[nat][:, None] ** 2 + freq[None, :] ** 2
        self.aperture_last = (9 * q2 < n * n).astype(np.float32)
        q2 = ky[:, None] ** 2 + kx[None, :] ** 2
        self.q2 = q2.astype(np.float32)
        self.aperture = (
            (9 * q2 < n * n) & ~((ky == 0) & second_y)[:, None] & ~((kx == 0) & second_x)[None, :]
        ).astype(np.float32)
        ay = 2.0 * np.pi / n * (np.outer(pix_y, np.arange(n)) % n)
        ax = 2.0 * np.pi / n * (np.outer(np.arange(n), pix_x) % n)
        self.start_y = np.stack(
            [
                np.concatenate([np.cos(ay), -np.sin(ay)], axis=1),
                np.concatenate([np.sin(ay), np.cos(ay)], axis=1),
            ]
        ) * scale
        self.start_x = np.stack(
            [
                np.concatenate([np.cos(ax), -np.sin(ax)], axis=0),
                np.concatenate([np.sin(ax), np.cos(ax)], axis=0),
            ]
        ) * scale


def dot(a, b):
    return jnp.dot(a, b, preferred_element_type=F32)


def gather_atoms(block, devices):
    steps = []
    step = 2
    while step < devices:
        steps.append(step)
        step *= 2
    for step in steps[:-1]:
        block = jnp.concatenate([block, swap(block, step, devices)], axis=0)
    if not steps:
        return [block]
    return [block, swap(block, steps[-1], devices)]


def swap(block, step, devices):
    return lax.ppermute(block, "probe", [(i, i ^ step) for i in range(devices)])


def sort_body(layers, species, pos_ref, kind_ref, layer_ref, kind_row_ref, layer_row_ref, out_ref, one_ref):
    rows = layer_ref.shape[0]
    count = rows * LANES
    owned = [(layer_ref[...] == s).astype(F32) for s in range(layers)]
    onehot = jnp.concatenate(owned, axis=0).astype(BF16)
    i = lax.broadcasted_iota(jnp.int32, (LANES, LANES), 0)
    j = lax.broadcasted_iota(jnp.int32, (LANES, LANES), 1)
    rank = dot(onehot, (i < j).astype(F32).astype(BF16))
    total = dot(onehot, jnp.ones((LANES, LANES), BF16)).astype(BF16)
    height = layers * rows
    i = lax.broadcasted_iota(jnp.int32, (height, height), 0)
    j = lax.broadcasted_iota(jnp.int32, (height, height), 1)
    rank = rank + dot((j < i).astype(F32).astype(BF16), total)
    place = jnp.zeros((rows, LANES), F32)
    for s in range(layers):
        place = place + owned[s] * rank[s * rows : (s + 1) * rows, :]
    place = place.astype(jnp.int32)
    sub = lax.broadcasted_iota(jnp.int32, (16, 2 * LANES), 0)
    for b in range(0, rows, 2):
        wanted = jnp.concatenate([place[b : b + 1, :], place[b + 1 : b + 2, :]], axis=1)
        for r in range(0, count, 16):
            hit = (sub + r == wanted).astype(F32).astype(BF16)
            one_ref[slice(r, r + 16), slice(b * LANES, (b + 2) * LANES)] = hit
    code = (kind_row_ref[...] + species * layer_row_ref[...]).astype(F32)
    values = jnp.concatenate([pos_ref[...], code], axis=0)
    high = values.astype(BF16).astype(F32)
    middle = (values - high).astype(BF16).astype(F32)
    low = (values - high) - middle
    parts = jnp.concatenate([high, middle, low], axis=0).astype(BF16)
    moved = lax.dot_general(parts, one_ref[...], (((1,), (1,)), ((), ())), preferred_element_type=F32)
    fields = values.shape[0]
    out_ref[0] = (moved[:fields] + moved[fields : 2 * fields]) + moved[2 * fields :]


def sort_atoms(positions, kind, layer, layers, species):
    count = kind.shape[0]
    rows = count // LANES

    def body(*refs):
        sort_body(layers, species, *refs)

    return pl.pallas_call(
        body,
        out_shape=jax.ShapeDtypeStruct((1, 3, count), F32),
        scratch_shapes=[pltpu.VMEM((count, count), BF16)],
        name="sort",
    )(
        positions,
        kind.reshape(rows, LANES),
        layer.reshape(rows, LANES),
        kind.reshape(1, count),
        layer.reshape(1, count),
    )


def build_body(layers, species, n, amp_ref, width_ref, *refs):
    *atom_refs, out_ref, gy_ref, gx_ref, acc_ref, all_ref, bound_ref, row_a, col_a, lay_a, row_b, col_b, lay_b = refs
    count = all_ref.shape[-1]
    chunks = count // LANES
    window = min(4, chunks)
    sub = lax.broadcasted_iota(jnp.int32, (16, LANES), 0)
    for h in range(G // n):
        for r in range(0, n, 16):
            rows = slice(h * n + r, h * n + r + 16)
            pixel = jnp.where(sub < 8, sub + r // 2, n + 7 - r // 2 - sub) + h * n
            gy_ref[rows, :] = pixel.astype(F32)
            pixel = jnp.where(sub + r < n // 2, sub + r, n + n // 2 - 1 - r - sub) + h * n
            gx_ref[rows, :] = pixel.astype(F32)
    filled = 0
    for ref in atom_refs:
        all_ref[filled : filled + ref.shape[0]] = ref[...]
        filled += ref.shape[0]

    segments = filled

    def find_bounds(segment, carry):
        layer = jnp.floor(all_ref[segment, 2:3, :] * (1.0 / species))
        bound_ref[segment, 0] = 0
        for s in range(1, layers):
            bound_ref[segment, s] = jnp.sum((layer < s).astype(F32)).astype(jnp.int32)
        bound_ref[segment, layers] = count
        return carry

    lax.fori_loop(0, segments, find_bounds, 0, unroll=min(segments, 8))

    def factors(segment, b, row_ref, col_ref, lay_ref):
        static = isinstance(b, int)
        lanes = slice(b * LANES, (b + 1) * LANES) if static else pl.ds(pl.multiple_of(b * LANES, LANES), LANES)
        code = all_ref[segment, 2:3, lanes]
        layer = jnp.floor(code * (1.0 / species))
        kind = code - layer * species
        a = jnp.zeros_like(code)
        w = jnp.ones_like(code)
        for k in range(species):
            a = jnp.where(kind == k, amp_ref[k], a)
            w = jnp.where(kind == k, width_ref[k], w)
        w = (-0.5 * math.log2(math.e)) / (w * w)
        lay_ref[b] = layer
        y = all_ref[segment, 0:1, lanes]
        x = all_ref[segment, 1:2, lanes]
        for r in range(0, G, 16):
            rows = slice(r, r + 16)
            d = gy_ref[rows, :] - y
            row_ref[b, rows, :] = (jnp.exp2(d * d * w) * a).astype(BF16)
            d = gx_ref[rows, :] - x
            col_ref[b, rows, :] = jnp.exp2(d * d * w).astype(BF16)

    def add_window(s, low, row_ref, col_ref, lay_ref):
        at = jnp.minimum(low, chunks - window)
        rows = []
        columns = []
        for k in range(window):
            mask = (lay_ref[at + k] == s) & (at + k >= low)
            rows.append(row_ref[at + k])
            columns.append(col_ref[at + k] * mask.astype(F32).astype(BF16))
        acc_ref[s] += lax.dot_general(
            jnp.concatenate(rows, axis=1),
            jnp.concatenate(columns, axis=1),
            (((1,), (1,)), ((), ())),
            preferred_element_type=F32,
        )

    acc_ref[...] = jnp.zeros_like(acc_ref)
    a_refs = (row_a, col_a, lay_a)
    b_refs = (row_b, col_b, lay_b)
    share = -(-chunks // layers)

    def low_of(segment, s):
        return bound_ref[segment, s] // LANES

    def all_factors(segment, refs):
        def one(b, carry):
            factors(segment, b, *refs)
            return carry

        lax.fori_loop(0, chunks, one, 0)

    def overlap(segment, refs, following, next_refs, over):
        for s in range(layers):
            low = low_of(segment, s)
            add_window(s, low, *refs)
            for b in range(s * share, min((s + 1) * share, chunks)):
                factors(following, b, *next_refs)
            over = jnp.maximum(over, bound_ref[segment, s + 1] - (low + window) * LANES)
        return over

    all_factors(0, a_refs)
    over = jnp.int32(0)
    last = segments - 1

    def pair(i, over):
        over = overlap(2 * i, a_refs, jnp.minimum(2 * i + 1, last), b_refs, over)
        return overlap(2 * i + 1, b_refs, jnp.minimum(2 * i + 2, last), a_refs, over)

    if segments > 1:
        over = lax.fori_loop(0, segments // 2, pair, over)
    else:
        over = overlap(0, a_refs, 0, b_refs, over)

    @pl.when(over > 0)
    def _():
        def segment_rest(segment, carry):
            all_factors(segment, a_refs)

            def slice_rest(s, carry):
                low = low_of(segment, s)
                chunk_end = (bound_ref[segment, s + 1] + LANES - 1) // LANES

                def more(t, carry):
                    add_window(s, low + t * window, *a_refs)
                    return carry

                return lax.fori_loop(1, (chunk_end - low + window - 1) // window, more, carry)

            return lax.fori_loop(0, layers, slice_rest, carry)

        lax.fori_loop(0, segments, segment_rest, 0)

    for s in range(layers):
        for r in range(0, G, 16):
            rows = slice(r, r + 16)
            out_ref[s, rows, :] = acc_ref[s, rows, :].astype(BF16)


def build(plan, atoms, amps, widths, layers):
    species = amps.shape[0]
    count = atoms[0].shape[-1]
    vmem = pl.BlockSpec(memory_space=pltpu.VMEM)
    smem = pl.BlockSpec(memory_space=pltpu.SMEM)

    def body(*refs):
        build_body(layers, species, plan.n, *refs)

    blocks = (count // LANES, G, LANES)
    buffers = [pltpu.VMEM(blocks, BF16), pltpu.VMEM(blocks, BF16), pltpu.VMEM((count // LANES, 1, LANES), F32)]
    return pl.pallas_call(
        body,
        out_shape=jax.ShapeDtypeStruct((layers, G, G), BF16),
        in_specs=[smem, smem] + [vmem] * len(atoms),
        out_specs=vmem,
        scratch_shapes=[
            pltpu.VMEM((G, LANES), F32),
            pltpu.VMEM((G, LANES), F32),
            pltpu.VMEM((layers, G, G), F32),
            pltpu.VMEM((sum(a.shape[0] for a in atoms), 3, count), F32),
            pltpu.SMEM((sum(a.shape[0] for a in atoms), layers + 1), jnp.int32),
        ]
        + buffers
        + buffers,
        name="build",
    )(amps, widths, *atoms)


def init_body(with_prop, *refs):
    if with_prop:
        shift_ref, phase_ref, spec_ref, ty_ref, tx_ref, q2_ref, ap_ref, z_ref, prop_ref, a_ref, b_ref = refs
        for layer in range(prop_ref.shape[0]):
            for r in range(0, q2_ref.shape[0], 16):
                rows = slice(r, r + 16)
                c, s = cos_sin(phase_ref[layer] * q2_ref[rows, :])
                prop_ref[layer, 0, rows, :] = ap_ref[rows, :] * c
                prop_ref[layer, 1, rows, :] = -(ap_ref[rows, :] * s)
    else:
        shift_ref, spec_ref, ty_ref, tx_ref, z_ref, a_ref, b_ref = refs
    n = spec_ref.shape[-1]
    positions = z_ref.shape[0]
    for p in range(positions):
        sy = shift_ref[p, 0]
        sx = shift_ref[p, 1]
        for r in range(0, n, 16):
            rows = slice(r, r + 16)
            ky = lax.broadcasted_iota(jnp.int32, (16, n), 0) + r
            kx = lax.broadcasted_iota(jnp.int32, (16, n), 1)
            turns = ((ky * sy + kx * sx) & (n - 1)).astype(F32) * (1.0 / n)
            c, s = cos_sin_turns(turns - jnp.round(turns))
            re = spec_ref[0, rows, :]
            im = spec_ref[1, rows, :]
            a_ref[p, rows, :] = (re * c + im * s).astype(BF16)
            a_ref[p, slice(n + r, n + r + 16), :] = (im * c - re * s).astype(BF16)
        b_ref[p, :, :n] = dot(ty_ref[0], a_ref[p]).astype(BF16)
        b_ref[p, :, n:] = dot(ty_ref[1], a_ref[p]).astype(BF16)
        z_ref[p, 0] = dot(b_ref[p], tx_ref[0])
        z_ref[p, 1] = dot(b_ref[p], tx_ref[1])


def init(plan, shifts, slice_phase, spectrum):
    n = plan.n
    positions = shifts.shape[0]
    vmem = pl.BlockSpec(memory_space=pltpu.VMEM)
    smem = pl.BlockSpec(memory_space=pltpu.SMEM)
    with_prop = slice_phase is not None
    tables = (jnp.asarray(plan.start_y, BF16), jnp.asarray(plan.start_x, BF16))
    waves = jax.ShapeDtypeStruct((positions, 2, n, n), F32)
    if with_prop:
        args = (shifts, slice_phase, spectrum, *tables, jnp.asarray(plan.q2), jnp.asarray(plan.aperture))
        specs = [smem, smem, vmem, vmem, vmem, vmem, vmem]
        out = (waves, jax.ShapeDtypeStruct((slice_phase.shape[0], 2, plan.rows, n), F32))
    else:
        args = (shifts, spectrum, *tables)
        specs = [smem, vmem, vmem, vmem]
        out = waves

    def body(*refs):
        init_body(with_prop, *refs)

    return pl.pallas_call(
        body,
        out_shape=out,
        in_specs=specs,
        out_specs=(vmem, vmem) if with_prop else vmem,
        scratch_shapes=[pltpu.VMEM((positions, 2 * n, n), BF16), pltpu.VMEM((positions, n, 2 * n), BF16)],
        name="init",
    )(*args)


def halves(x, axis):
    h = x.shape[axis] // 2
    if axis == 0:
        return x[:h], x[h:]
    return x[:, :h], x[:, h:]


def forward_pair(re, im, axis):
    rt, rb = halves(re, axis)
    it, ib = halves(im, axis)
    u = jnp.concatenate([rt + rb, it - ib], axis=axis)
    w = jnp.concatenate([it + ib, rb - rt], axis=axis)
    return u.astype(BF16), w.astype(BF16)


def inverse_pair(re, im, axis):
    rt, rb = halves(re, axis)
    it, ib = halves(im, axis)
    u = jnp.concatenate([rt + rb, ib - it], axis=axis)
    w = jnp.concatenate([it + ib, rt - rb], axis=axis)
    return u.astype(BF16), w.astype(BF16)


def slice_body(plan, direct, off_ref, own_ref, got_ref, za_ref, zb_ref, prop_ref, fy_ref, fx_ref, iy_ref, ix_ref,
               ly_ref, lx_ref, la_ref, out_ref, part_ref, v_ref, z_ref, u_ref, y_ref, t_ref, x_ref, sem, wave_sem):
    n = plan.n
    rows_f = plan.rows
    half = za_ref.shape[0]
    positions = half + zb_ref.shape[0]
    layers = own_ref.shape[0]

    def fetch(layer):
        return [
            pltpu.make_async_copy(own_ref.at[layer], part_ref.at[0, layer], sem.at[0, layer]),
            pltpu.make_async_copy(got_ref.at[layer], part_ref.at[1, layer], sem.at[1, layer]),
        ]

    waves = [
        pltpu.make_async_copy(za_ref, z_ref.at[:half], wave_sem.at[0]),
        pltpu.make_async_copy(zb_ref, z_ref.at[half:], wave_sem.at[1]),
    ]
    for copy in fetch(0):
        copy.start()
    for copy in waves:
        copy.start()
    for layer in range(1, layers):
        for copy in fetch(layer):
            copy.start()

    def combine(layer):
        for copy in fetch(layer):
            copy.wait()
        for r in range(0, G, 16):
            rows = slice(r, r + 16)
            total = part_ref[0, layer, rows, :].astype(F32) + part_ref[1, layer, rows, :].astype(F32)
            v_ref[rows, :] = total.astype(BF16).astype(F32)

    lane = lax.broadcasted_iota(jnp.int32, (16, n), 1)
    pixel_x = jnp.where(lane < n // 2, lane, n + n // 2 - 1 - lane)
    sub = lax.broadcasted_iota(jnp.int32, (16, n), 0)

    def transmit(p):
        oy = off_ref[p, 0]
        ox = off_ref[p, 1]
        inside_x = pixel_x >= ox
        for g in range(n // 16):
            rows = slice(16 * g, 16 * g + 16)
            far = slice(n + 16 * g, n + 16 * g + 16)
            pixel_y = jnp.where(sub < 8, sub + 8 * g, n + 7 - 8 * g - sub)
            near_v = jnp.where(inside_x, v_ref[rows, :n], v_ref[rows, n:])
            far_v = jnp.where(inside_x, v_ref[far, :n], v_ref[far, n:])
            c, s = cos_sin(jnp.where(pixel_y >= oy, near_v, far_v))
            zr = z_ref[p, 0, rows, :]
            zi = z_ref[p, 1, rows, :]
            u, w = forward_pair(zr * c - zi * s, zr * s + zi * c, 0)
            u_ref[p, 0, rows, :] = u
            u_ref[p, 1, rows, :] = w

    spans = [
        (slice(16 * g, 16 * g + 16), slice(rows_f + 16 * g, rows_f + 16 * g + 16))
        for g in range(rows_f // 16)
    ]

    def forward_rows(p, layer):
        y_ref[p, 0, :rows_f] = dot(fy_ref[...], u_ref[p, 0])
        y_ref[p, 1, :rows_f] = dot(fy_ref[...], u_ref[p, 1])

    def pair_columns(p, layer):
        for rows, low in spans:
            t_ref[p, rows, :], t_ref[p, low, :] = forward_pair(y_ref[p, 0, rows, :], y_ref[p, 1, rows, :], 1)

    def forward_columns(p, layer):
        x_ref[p, : 2 * rows_f] = dot(t_ref[p, : 2 * rows_f], fx_ref[...])

    def propagate(p, layer):
        for rows, low in spans:
            re = x_ref[p, rows, :]
            im = x_ref[p, low, :]
            pr = prop_ref[layer, 0, rows, :]
            pi = prop_ref[layer, 1, rows, :]
            t_ref[p, rows, :], t_ref[p, low, :] = inverse_pair(re * pr - im * pi, re * pi + im * pr, 1)

    def inverse_columns(p, layer):
        x_ref[p, : 2 * rows_f] = dot(t_ref[p, : 2 * rows_f], ix_ref[...])

    def pair_rows(p, layer):
        for rows, low in spans:
            t_ref[p, rows, :], t_ref[p, low, :] = inverse_pair(x_ref[p, rows, :], x_ref[p, low, :], 0)

    def inverse_rows(p, layer):
        z_ref[p, 0] = dot(iy_ref[...], t_ref[p, :rows_f])
        z_ref[p, 1] = dot(iy_ref[...], t_ref[p, rows_f : 2 * rows_f])

    stages = [
        lambda p, layer: transmit(p),
        forward_rows,
        pair_columns,
        forward_columns,
        propagate,
        inverse_columns,
        pair_rows,
        inverse_rows,
    ]
    def in_turn(steps, layer):
        for t in range(len(steps) + positions - 1):
            for p in range(positions):
                if 0 <= t - p < len(steps):
                    steps[t - p](p, layer)

    def step(layer, carry):
        combine(layer)
        in_turn(stages, layer)
        return carry

    for copy in waves:
        copy.wait()
    lax.fori_loop(0, layers - 1, step, 0)
    combine(layers - 1)
    keep = plan.keep
    count = 2 * keep

    def last_rows(p, layer):
        y_ref[p, 0] = dot(ly_ref[...], u_ref[p, 0])
        y_ref[p, 1] = dot(ly_ref[...], u_ref[p, 1])

    def last_pairs(p, layer):
        for g in range(count // 16):
            rows = slice(16 * g, 16 * g + 16)
            low = slice(count + 16 * g, count + 16 * g + 16)
            t_ref[p, rows, :], t_ref[p, low, :] = forward_pair(y_ref[p, 0, rows, :], y_ref[p, 1, rows, :], 1)

    def last_columns(p, layer):
        x_ref[p] = dot(t_ref[p], lx_ref[...])

    def intensity(p, layer):
        for g in range(n // 16):
            r = 16 * g
            if r < keep:
                src = r
            elif r >= n - keep:
                src = r - (n - count)
            else:
                src = None
            if src is None:
                value = jnp.zeros((16, n), BF16)
            else:
                re = x_ref[p, slice(src, src + 16), :]
                im = x_ref[p, slice(count + src, count + src + 16), :]
                value = (la_ref[slice(src, src + 16), :] * (re * re + im * im)).astype(BF16)
            if direct:
                out_ref[g, p] = value
            else:
                out_ref[p, slice(r, r + 16), :] = value

    in_turn([stages[0], last_rows, last_pairs, last_columns, intensity], layers - 1)


def multislice(plan, offsets, own, got, start, prop, direct):
    n = plan.n
    positions = offsets.shape[0]
    vmem = pl.BlockSpec(memory_space=pltpu.VMEM)
    smem = pl.BlockSpec(memory_space=pltpu.SMEM)
    anywhere = pl.BlockSpec(memory_space=pl.ANY)
    shape = (n // 16, positions, 16, n) if direct else (positions, n, n)
    count = 2 * plan.keep

    def body(*refs):
        slice_body(plan, direct, *refs)

    return pl.pallas_call(
        body,
        out_shape=jax.ShapeDtypeStruct(shape, BF16),
        in_specs=[smem] + [anywhere] * 4 + [vmem] * 8,
        out_specs=vmem,
        scratch_shapes=[
            pltpu.VMEM((2,) + own.shape, BF16),
            pltpu.VMEM((G, G), F32),
            pltpu.VMEM((positions, 2, n, n), F32),
            pltpu.VMEM((positions, 2, n, n), BF16),
            pltpu.VMEM((positions, 2, count, n), F32),
            pltpu.VMEM((positions, 2 * count, n), BF16),
            pltpu.VMEM((positions, 2 * count, n), F32),
            pltpu.SemaphoreType.DMA((2, own.shape[0])),
            pltpu.SemaphoreType.DMA((2,)),
        ],
        name="multislice",
    )(
        offsets,
        own,
        got,
        *start,
        prop,
        jnp.asarray(plan.fwd_y, BF16),
        jnp.asarray(plan.fwd_x, BF16),
        jnp.asarray(plan.inv_y, BF16),
        jnp.asarray(plan.inv_x, BF16),
        jnp.asarray(plan.last_y, BF16),
        jnp.asarray(plan.last_x, BF16),
        jnp.asarray(plan.aperture_last),
    )


def scan_matrix(positions):
    index = np.arange(positions)
    angle = 2.0 * np.pi / positions * (np.outer(index, index) % positions)
    return np.concatenate([np.cos(angle), -np.sin(angle)]) / math.sqrt(positions)


def on_device(
    atom_positions,
    atom_species,
    atom_slice,
    species_amp,
    species_width,
    probe_spectrum,
    window_offsets,
    probe_shifts,
    slice_phase,
):
    devices = lax.axis_size("probe")
    n = probe_spectrum.shape[-1]
    layers = slice_phase.shape[0] + 1
    plan = Plan(n)
    species = species_amp.shape[0]
    atoms = sort_atoms(atom_positions, atom_species, atom_slice, layers, species)
    atoms = gather_atoms(atoms, devices)
    shifts = (probe_shifts + window_offsets) & (n - 1)
    half = -(-shifts.shape[0] // 4)
    start_a, prop = init(plan, shifts[:half], slice_phase, probe_spectrum)
    *atoms, start_a, prop = lax.optimization_barrier((*atoms, start_a, prop))
    own = build(plan, atoms, species_amp, species_width, layers)
    got = swap(own, 1, devices)
    shifts, own = lax.optimization_barrier((shifts[half:], own))
    start_b = init(plan, shifts, None, probe_spectrum)
    rows = n // devices
    direct = rows % 16 == 0
    intensity = multislice(plan, window_offsets, own, got, (start_a, start_b), prop, direct)
    positions = window_offsets.shape[0]
    if direct:
        received = lax.all_to_all(intensity, "probe", split_axis=0, concat_axis=0, tiled=True)
    else:
        pieces = intensity.reshape(positions, devices, rows, n)
        received = lax.all_to_all(pieces, "probe", split_axis=1, concat_axis=0, tiled=True)
    count = positions * devices
    received = received.reshape(count, rows * n)
    product = dot(jnp.asarray(scan_matrix(count), BF16), received)
    return product.reshape(2, count, rows * n)


def solution(mesh):
    placed = (
        P(None, ("groups", "probe")),
        P(("groups", "probe")),
        P(("groups", "probe")),
        P(),
        P(),
        P(),
        P(("groups", "probe"), None),
        P(("groups", "probe"), None),
        P(),
    )
    return jax.shard_map(
        on_device, mesh=mesh, in_specs=placed, out_specs=P(None, "groups", "probe"), check_vma=False
    )
```

```python
import math

import jax
import jax.numpy as jnp
import numpy as np
from jax import lax
from jax.experimental import pallas as pl
from jax.experimental.pallas import tpu as pltpu
from jax.sharding import PartitionSpec as P

G = 512
LANES = 128
BF16 = jnp.bfloat16
F32 = jnp.float32


def sine_fit():
    nodes = 0.125 * (1.0 - np.cos((np.arange(400) + 0.5) * np.pi / 400))
    f = np.sqrt(nodes)
    fit = np.polynomial.chebyshev.Chebyshev.fit(nodes, np.sin(np.pi * f) / f, 4, domain=[0.0, 0.25])
    return [float(c) for c in fit.convert(kind=np.polynomial.Polynomial).coef]


SIN_FIT = sine_fit()
TURN_HIGH = float(np.float32(np.round(2.0**16 / (2.0 * np.pi)) / 2.0**16))
TURN_LOW = float(1.0 / (2.0 * np.pi) - TURN_HIGH)


def horner(coefficients, g):
    total = coefficients[-1]
    for c in coefficients[-2::-1]:
        total = total * g + c
    return total


def cos_sin_turns(f):
    sine = f * horner(SIN_FIT, f * f)
    square = sine * sine
    cosine_square = jnp.maximum(1.0 - square, 1e-30)
    return (1.0 - 2.0 * square, 2.0 * sine * (cosine_square * lax.rsqrt(cosine_square)))


def cos_sin(v):
    t = v * TURN_HIGH
    return cos_sin_turns((t - jnp.round(t)) + v * TURN_LOW)


def mirrored(length, tile):
    m = np.arange(length // 2).reshape(-1, tile)
    return np.concatenate([m, length - 1 - m], axis=1).reshape(-1)


def signed(half, tile):
    m = np.arange(half).reshape(-1, tile)
    k = np.concatenate([m, -m], axis=1).reshape(-1)
    second = np.concatenate([np.zeros_like(m), np.ones_like(m)], axis=1).reshape(-1) == 1
    return k, second


class Plan:
    def __init__(self, length):
        n = self.n = length
        kmax = max(k for k in range(n) if 9 * k * k < n * n)
        self.half_y = -(-(kmax + 1) // 8) * 8
        self.rows = 2 * self.half_y
        pix_y = mirrored(n, 8)
        pix_x = mirrored(n, n // 2)
        ky, second_y = signed(self.half_y, 8)
        kx, second_x = signed(n // 2, n // 2)
        scale = 1.0 / math.sqrt(n)

        def forward(freq, pix, odd_slot):
            m = np.where(odd_slot, n - 1 - pix, pix)
            angle = 2.0 * np.pi / n * np.outer(freq, m + 0.5)
            return np.where(odd_slot[None, :], np.sin(angle), np.cos(angle)) * scale

        odd_y = pix_y >= n // 2
        odd_x = pix_x >= n // 2
        self.fwd_y = forward(ky, pix_y, odd_y)
        self.fwd_x = forward(kx, pix_x, odd_x).T

        def inverse(pix, freq, second):
            angle = 2.0 * np.pi / n * np.outer(pix + 0.5, np.abs(freq))
            return np.where(second[None, :], np.sin(angle), np.cos(angle)) * scale

        self.inv_y = inverse(pix_y, ky, second_y)
        self.inv_x = inverse(pix_x, kx, second_x).T
        block = 16
        keep = -(-(kmax + 1) // block) * block
        self.keep = keep
        nat = np.concatenate([np.arange(keep), np.arange(n - keep, n)])
        self.last_y = forward(nat, pix_y, odd_y)
        self.last_x = forward(np.arange(n), pix_x, odd_x).T
        freq = (np.arange(n) + n // 2) % n - n // 2
        q2 = freq[nat][:, None] ** 2 + freq[None, :] ** 2
        self.aperture_last = (9 * q2 < n * n).astype(np.float32)
        q2 = ky[:, None] ** 2 + kx[None, :] ** 2
        self.q2 = q2.astype(np.float32)
        self.aperture = (
            (9 * q2 < n * n) & ~((ky == 0) & second_y)[:, None] & ~((kx == 0) & second_x)[None, :]
        ).astype(np.float32)
        ay = 2.0 * np.pi / n * (np.outer(pix_y, np.arange(n)) % n)
        ax = 2.0 * np.pi / n * (np.outer(np.arange(n), pix_x) % n)
        self.start_y = np.stack(
            [
                np.concatenate([np.cos(ay), -np.sin(ay)], axis=1),
                np.concatenate([np.sin(ay), np.cos(ay)], axis=1),
            ]
        ) * scale
        self.start_x = np.stack(
            [
                np.concatenate([np.cos(ax), -np.sin(ax)], axis=0),
                np.concatenate([np.sin(ax), np.cos(ax)], axis=0),
            ]
        ) * scale


def dot(a, b):
    return jnp.dot(a, b, preferred_element_type=F32)


def gather_atoms(block, devices):
    steps = []
    step = 2
    while step < devices:
        steps.append(step)
        step *= 2
    for step in steps[:-1]:
        block = jnp.concatenate([block, swap(block, step, devices)], axis=0)
    if not steps:
        return [block]
    return [block, swap(block, steps[-1], devices)]


def swap(block, step, devices):
    return lax.ppermute(block, "probe", [(i, i ^ step) for i in range(devices)])


def sort_body(layers, species, pos_ref, kind_ref, layer_ref, kind_row_ref, layer_row_ref, out_ref, one_ref):
    rows = layer_ref.shape[0]
    count = rows * LANES
    owned = [(layer_ref[...] == s).astype(F32) for s in range(layers)]
    onehot = jnp.concatenate(owned, axis=0).astype(BF16)
    i = lax.broadcasted_iota(jnp.int32, (LANES, LANES), 0)
    j = lax.broadcasted_iota(jnp.int32, (LANES, LANES), 1)
    rank = dot(onehot, (i < j).astype(F32).astype(BF16))
    total = dot(onehot, jnp.ones((LANES, LANES), BF16)).astype(BF16)
    height = layers * rows
    i = lax.broadcasted_iota(jnp.int32, (height, height), 0)
    j = lax.broadcasted_iota(jnp.int32, (height, height), 1)
    rank = rank + dot((j < i).astype(F32).astype(BF16), total)
    place = jnp.zeros((rows, LANES), F32)
    for s in range(layers):
        place = place + owned[s] * rank[s * rows : (s + 1) * rows, :]
    place = place.astype(jnp.int32)
    sub = lax.broadcasted_iota(jnp.int32, (16, 2 * LANES), 0)
    for b in range(0, rows, 2):
        wanted = jnp.concatenate([place[b : b + 1, :], place[b + 1 : b + 2, :]], axis=1)
        for r in range(0, count, 16):
            hit = (sub + r == wanted).astype(F32).astype(BF16)
            one_ref[slice(r, r + 16), slice(b * LANES, (b + 2) * LANES)] = hit
    code = (kind_row_ref[...] + species * layer_row_ref[...]).astype(F32)
    values = jnp.concatenate([pos_ref[...], code], axis=0)
    high = values.astype(BF16).astype(F32)
    middle = (values - high).astype(BF16).astype(F32)
    low = (values - high) - middle
    parts = jnp.concatenate([high, middle, low], axis=0).astype(BF16)
    moved = lax.dot_general(parts, one_ref[...], (((1,), (1,)), ((), ())), preferred_element_type=F32)
    fields = values.shape[0]
    out_ref[0] = (moved[:fields] + moved[fields : 2 * fields]) + moved[2 * fields :]


def sort_atoms(positions, kind, layer, layers, species):
    count = kind.shape[0]
    rows = count // LANES

    def body(*refs):
        sort_body(layers, species, *refs)

    return pl.pallas_call(
        body,
        out_shape=jax.ShapeDtypeStruct((1, 3, count), F32),
        scratch_shapes=[pltpu.VMEM((count, count), BF16)],
        name="sort",
    )(
        positions,
        kind.reshape(rows, LANES),
        layer.reshape(rows, LANES),
        kind.reshape(1, count),
        layer.reshape(1, count),
    )


def build_body(layers, species, n, amp_ref, width_ref, *refs):
    *atom_refs, out_ref, gy_ref, gx_ref, acc_ref, all_ref, bound_ref, row_a, col_a, lay_a, row_b, col_b, lay_b = refs
    count = all_ref.shape[-1]
    chunks = count // LANES
    window = min(4, chunks)
    sub = lax.broadcasted_iota(jnp.int32, (16, LANES), 0)
    for h in range(G // n):
        for r in range(0, n, 16):
            rows = slice(h * n + r, h * n + r + 16)
            pixel = jnp.where(sub < 8, sub + r // 2, n + 7 - r // 2 - sub) + h * n
            gy_ref[rows, :] = pixel.astype(F32)
            pixel = jnp.where(sub + r < n // 2, sub + r, n + n // 2 - 1 - r - sub) + h * n
            gx_ref[rows, :] = pixel.astype(F32)
    filled = 0
    for ref in atom_refs:
        all_ref[filled : filled + ref.shape[0]] = ref[...]
        filled += ref.shape[0]

    segments = filled

    def find_bounds(segment, carry):
        layer = jnp.floor(all_ref[segment, 2:3, :] * (1.0 / species))
        bound_ref[segment, 0] = 0
        for s in range(1, layers):
            bound_ref[segment, s] = jnp.sum((layer < s).astype(F32)).astype(jnp.int32)
        bound_ref[segment, layers] = count
        return carry

    lax.fori_loop(0, segments, find_bounds, 0, unroll=min(segments, 8))

    def factors(segment, b, row_ref, col_ref, lay_ref):
        static = isinstance(b, int)
        lanes = slice(b * LANES, (b + 1) * LANES) if static else pl.ds(pl.multiple_of(b * LANES, LANES), LANES)
        code = all_ref[segment, 2:3, lanes]
        layer = jnp.floor(code * (1.0 / species))
        kind = code - layer * species
        a = jnp.zeros_like(code)
        w = jnp.ones_like(code)
        for k in range(species):
            a = jnp.where(kind == k, amp_ref[k], a)
            w = jnp.where(kind == k, width_ref[k], w)
        w = (-0.5 * math.log2(math.e)) / (w * w)
        lay_ref[b] = layer
        y = all_ref[segment, 0:1, lanes]
        x = all_ref[segment, 1:2, lanes]
        for r in range(0, G, 16):
            rows = slice(r, r + 16)
            d = gy_ref[rows, :] - y
            row_ref[b, rows, :] = (jnp.exp2(d * d * w) * a).astype(BF16)
            d = gx_ref[rows, :] - x
            col_ref[b, rows, :] = jnp.exp2(d * d * w).astype(BF16)

    def add_window(s, low, row_ref, col_ref, lay_ref):
        at = jnp.minimum(low, chunks - window)
        rows = []
        columns = []
        for k in range(window):
            mask = (lay_ref[at + k] == s) & (at + k >= low)
            rows.append(row_ref[at + k])
            columns.append(col_ref[at + k] * mask.astype(F32).astype(BF16))
        acc_ref[s] += lax.dot_general(
            jnp.concatenate(rows, axis=1),
            jnp.concatenate(columns, axis=1),
            (((1,), (1,)), ((), ())),
            preferred_element_type=F32,
        )

    acc_ref[...] = jnp.zeros_like(acc_ref)
    a_refs = (row_a, col_a, lay_a)
    b_refs = (row_b, col_b, lay_b)
    share = -(-chunks // layers)

    def low_of(segment, s):
        return bound_ref[segment, s] // LANES

    def all_factors(segment, refs):
        def one(b, carry):
            factors(segment, b, *refs)
            return carry

        lax.fori_loop(0, chunks, one, 0)

    def overlap(segment, refs, following, next_refs, over):
        for s in range(layers):
            low = low_of(segment, s)
            add_window(s, low, *refs)
            for b in range(s * share, min((s + 1) * share, chunks)):
                factors(following, b, *next_refs)
            over = jnp.maximum(over, bound_ref[segment, s + 1] - (low + window) * LANES)
        return over

    all_factors(0, a_refs)
    over = jnp.int32(0)
    last = segments - 1

    def pair(i, over):
        over = overlap(2 * i, a_refs, jnp.minimum(2 * i + 1, last), b_refs, over)
        return overlap(2 * i + 1, b_refs, jnp.minimum(2 * i + 2, last), a_refs, over)

    if segments > 1:
        over = lax.fori_loop(0, segments // 2, pair, over)
    else:
        over = overlap(0, a_refs, 0, b_refs, over)

    @pl.when(over > 0)
    def _():
        def segment_rest(segment, carry):
            all_factors(segment, a_refs)

            def slice_rest(s, carry):
                low = low_of(segment, s)
                chunk_end = (bound_ref[segment, s + 1] + LANES - 1) // LANES

                def more(t, carry):
                    add_window(s, low + t * window, *a_refs)
                    return carry

                return lax.fori_loop(1, (chunk_end - low + window - 1) // window, more, carry)

            return lax.fori_loop(0, layers, slice_rest, carry)

        lax.fori_loop(0, segments, segment_rest, 0)

    for s in range(layers):
        for r in range(0, G, 16):
            rows = slice(r, r + 16)
            out_ref[s, rows, :] = acc_ref[s, rows, :].astype(BF16)


def build(plan, atoms, amps, widths, layers):
    species = amps.shape[0]
    count = atoms[0].shape[-1]
    vmem = pl.BlockSpec(memory_space=pltpu.VMEM)
    smem = pl.BlockSpec(memory_space=pltpu.SMEM)

    def body(*refs):
        build_body(layers, species, plan.n, *refs)

    blocks = (count // LANES, G, LANES)
    buffers = [pltpu.VMEM(blocks, BF16), pltpu.VMEM(blocks, BF16), pltpu.VMEM((count // LANES, 1, LANES), F32)]
    return pl.pallas_call(
        body,
        out_shape=jax.ShapeDtypeStruct((layers, G, G), BF16),
        in_specs=[smem, smem] + [vmem] * len(atoms),
        out_specs=vmem,
        scratch_shapes=[
            pltpu.VMEM((G, LANES), F32),
            pltpu.VMEM((G, LANES), F32),
            pltpu.VMEM((layers, G, G), F32),
            pltpu.VMEM((sum(a.shape[0] for a in atoms), 3, count), F32),
            pltpu.SMEM((sum(a.shape[0] for a in atoms), layers + 1), jnp.int32),
        ]
        + buffers
        + buffers,
        name="build",
    )(amps, widths, *atoms)


def init_body(with_prop, *refs):
    if with_prop:
        shift_ref, phase_ref, spec_ref, ty_ref, tx_ref, q2_ref, ap_ref, z_ref, prop_ref, a_ref, b_ref = refs
        for layer in range(prop_ref.shape[0]):
            for r in range(0, q2_ref.shape[0], 16):
                rows = slice(r, r + 16)
                c, s = cos_sin(phase_ref[layer] * q2_ref[rows, :])
                prop_ref[layer, 0, rows, :] = ap_ref[rows, :] * c
                prop_ref[layer, 1, rows, :] = -(ap_ref[rows, :] * s)
    else:
        shift_ref, spec_ref, ty_ref, tx_ref, z_ref, a_ref, b_ref = refs
    n = spec_ref.shape[-1]
    positions = z_ref.shape[0]

    def phases(p):
        sy = shift_ref[p, 0]
        sx = shift_ref[p, 1]
        for r in range(0, n, 16):
            rows = slice(r, r + 16)
            ky = lax.broadcasted_iota(jnp.int32, (16, n), 0) + r
            kx = lax.broadcasted_iota(jnp.int32, (16, n), 1)
            turns = ((ky * sy + kx * sx) & (n - 1)).astype(F32) * (1.0 / n)
            c, s = cos_sin_turns(turns - jnp.round(turns))
            re = spec_ref[0, rows, :]
            im = spec_ref[1, rows, :]
            a_ref[p, rows, :] = (re * c + im * s).astype(BF16)
            a_ref[p, slice(n + r, n + r + 16), :] = (im * c - re * s).astype(BF16)

    def along_y(p):
        b_ref[p, :, :n] = dot(ty_ref[0], a_ref[p]).astype(BF16)
        b_ref[p, :, n:] = dot(ty_ref[1], a_ref[p]).astype(BF16)

    def along_x(p):
        z_ref[p, 0] = dot(b_ref[p], tx_ref[0])
        z_ref[p, 1] = dot(b_ref[p], tx_ref[1])

    steps = [phases, along_y, along_x]
    for t in range(len(steps) + positions - 1):
        for p in range(positions):
            if 0 <= t - p < len(steps):
                steps[t - p](p)


def init(plan, shifts, slice_phase, spectrum):
    n = plan.n
    positions = shifts.shape[0]
    vmem = pl.BlockSpec(memory_space=pltpu.VMEM)
    smem = pl.BlockSpec(memory_space=pltpu.SMEM)
    with_prop = slice_phase is not None
    tables = (jnp.asarray(plan.start_y, BF16), jnp.asarray(plan.start_x, BF16))
    waves = jax.ShapeDtypeStruct((positions, 2, n, n), F32)
    if with_prop:
        args = (shifts, slice_phase, spectrum, *tables, jnp.asarray(plan.q2), jnp.asarray(plan.aperture))
        specs = [smem, smem, vmem, vmem, vmem, vmem, vmem]
        out = (waves, jax.ShapeDtypeStruct((slice_phase.shape[0], 2, plan.rows, n), F32))
    else:
        args = (shifts, spectrum, *tables)
        specs = [smem, vmem, vmem, vmem]
        out = waves

    def body(*refs):
        init_body(with_prop, *refs)

    return pl.pallas_call(
        body,
        out_shape=out,
        in_specs=specs,
        out_specs=(vmem, vmem) if with_prop else vmem,
        scratch_shapes=[pltpu.VMEM((positions, 2 * n, n), BF16), pltpu.VMEM((positions, n, 2 * n), BF16)],
        name="init",
    )(*args)


def halves(x, axis):
    h = x.shape[axis] // 2
    if axis == 0:
        return x[:h], x[h:]
    return x[:, :h], x[:, h:]


def forward_pair(re, im, axis):
    rt, rb = halves(re, axis)
    it, ib = halves(im, axis)
    u = jnp.concatenate([rt + rb, it - ib], axis=axis)
    w = jnp.concatenate([it + ib, rb - rt], axis=axis)
    return u.astype(BF16), w.astype(BF16)


def inverse_pair(re, im, axis):
    rt, rb = halves(re, axis)
    it, ib = halves(im, axis)
    u = jnp.concatenate([rt + rb, ib - it], axis=axis)
    w = jnp.concatenate([it + ib, rt - rb], axis=axis)
    return u.astype(BF16), w.astype(BF16)


def slice_body(plan, direct, off_ref, own_ref, got_ref, za_ref, zb_ref, prop_ref, fy_ref, fx_ref, iy_ref, ix_ref,
               ly_ref, lx_ref, la_ref, out_ref, part_ref, v_ref, z_ref, u_ref, y_ref, t_ref, x_ref, sem, wave_sem):
    n = plan.n
    rows_f = plan.rows
    half = za_ref.shape[0]
    positions = half + zb_ref.shape[0]
    layers = own_ref.shape[0]

    def fetch(layer):
        return [
            pltpu.make_async_copy(own_ref.at[layer], part_ref.at[0, layer], sem.at[0, layer]),
            pltpu.make_async_copy(got_ref.at[layer], part_ref.at[1, layer], sem.at[1, layer]),
        ]

    waves = [
        pltpu.make_async_copy(za_ref, z_ref.at[:half], wave_sem.at[0]),
        pltpu.make_async_copy(zb_ref, z_ref.at[half:], wave_sem.at[1]),
    ]
    for copy in fetch(0):
        copy.start()
    for copy in waves:
        copy.start()
    for layer in range(1, layers):
        for copy in fetch(layer):
            copy.start()

    def combine(layer):
        for copy in fetch(layer):
            copy.wait()
        for r in range(0, G, 16):
            rows = slice(r, r + 16)
            total = part_ref[0, layer, rows, :].astype(F32) + part_ref[1, layer, rows, :].astype(F32)
            v_ref[rows, :] = total.astype(BF16).astype(F32)

    lane = lax.broadcasted_iota(jnp.int32, (16, n), 1)
    pixel_x = jnp.where(lane < n // 2, lane, n + n // 2 - 1 - lane)
    sub = lax.broadcasted_iota(jnp.int32, (16, n), 0)

    def transmit(p):
        oy = off_ref[p, 0]
        ox = off_ref[p, 1]
        inside_x = pixel_x >= ox
        for g in range(n // 16):
            rows = slice(16 * g, 16 * g + 16)
            far = slice(n + 16 * g, n + 16 * g + 16)
            pixel_y = jnp.where(sub < 8, sub + 8 * g, n + 7 - 8 * g - sub)
            near_v = jnp.where(inside_x, v_ref[rows, :n], v_ref[rows, n:])
            far_v = jnp.where(inside_x, v_ref[far, :n], v_ref[far, n:])
            c, s = cos_sin(jnp.where(pixel_y >= oy, near_v, far_v))
            zr = z_ref[p, 0, rows, :]
            zi = z_ref[p, 1, rows, :]
            u, w = forward_pair(zr * c - zi * s, zr * s + zi * c, 0)
            u_ref[p, 0, rows, :] = u
            u_ref[p, 1, rows, :] = w

    spans = [
        (slice(16 * g, 16 * g + 16), slice(rows_f + 16 * g, rows_f + 16 * g + 16))
        for g in range(rows_f // 16)
    ]

    def forward_rows(p, layer):
        y_ref[p, 0, :rows_f] = dot(fy_ref[...], u_ref[p, 0])
        y_ref[p, 1, :rows_f] = dot(fy_ref[...], u_ref[p, 1])

    def pair_columns(p, layer):
        for rows, low in spans:
            t_ref[p, rows, :], t_ref[p, low, :] = forward_pair(y_ref[p, 0, rows, :], y_ref[p, 1, rows, :], 1)

    def forward_columns(p, layer):
        x_ref[p, : 2 * rows_f] = dot(t_ref[p, : 2 * rows_f], fx_ref[...])

    def propagate(p, layer):
        for rows, low in spans:
            re = x_ref[p, rows, :]
            im = x_ref[p, low, :]
            pr = prop_ref[layer, 0, rows, :]
            pi = prop_ref[layer, 1, rows, :]
            t_ref[p, rows, :], t_ref[p, low, :] = inverse_pair(re * pr - im * pi, re * pi + im * pr, 1)

    def inverse_columns(p, layer):
        x_ref[p, : 2 * rows_f] = dot(t_ref[p, : 2 * rows_f], ix_ref[...])

    def pair_rows(p, layer):
        for rows, low in spans:
            t_ref[p, rows, :], t_ref[p, low, :] = inverse_pair(x_ref[p, rows, :], x_ref[p, low, :], 0)

    def inverse_rows(p, layer):
        z_ref[p, 0] = dot(iy_ref[...], t_ref[p, :rows_f])
        z_ref[p, 1] = dot(iy_ref[...], t_ref[p, rows_f : 2 * rows_f])

    stages = [
        lambda p, layer: transmit(p),
        forward_rows,
        pair_columns,
        forward_columns,
        propagate,
        inverse_columns,
        pair_rows,
        inverse_rows,
    ]
    def in_turn(steps, layer):
        for t in range(len(steps) + positions - 1):
            for p in range(positions):
                if 0 <= t - p < len(steps):
                    steps[t - p](p, layer)

    def step(layer, carry):
        combine(layer)
        in_turn(stages, layer)
        return carry

    for copy in waves:
        copy.wait()
    lax.fori_loop(0, layers - 1, step, 0)
    combine(layers - 1)
    keep = plan.keep
    count = 2 * keep

    def last_rows(p, layer):
        y_ref[p, 0] = dot(ly_ref[...], u_ref[p, 0])
        y_ref[p, 1] = dot(ly_ref[...], u_ref[p, 1])

    def last_pairs(p, layer):
        for g in range(count // 16):
            rows = slice(16 * g, 16 * g + 16)
            low = slice(count + 16 * g, count + 16 * g + 16)
            t_ref[p, rows, :], t_ref[p, low, :] = forward_pair(y_ref[p, 0, rows, :], y_ref[p, 1, rows, :], 1)

    def last_columns(p, layer):
        x_ref[p] = dot(t_ref[p], lx_ref[...])

    def intensity(p, layer):
        for g in range(n // 16):
            r = 16 * g
            if r < keep:
                src = r
            elif r >= n - keep:
                src = r - (n - count)
            else:
                src = None
            if src is None:
                value = jnp.zeros((16, n), BF16)
            else:
                re = x_ref[p, slice(src, src + 16), :]
                im = x_ref[p, slice(count + src, count + src + 16), :]
                value = (la_ref[slice(src, src + 16), :] * (re * re + im * im)).astype(BF16)
            if direct:
                out_ref[g, p] = value
            else:
                out_ref[p, slice(r, r + 16), :] = value

    in_turn([stages[0], last_rows, last_pairs, last_columns, intensity], layers - 1)


def multislice(plan, offsets, own, got, start, prop, direct):
    n = plan.n
    positions = offsets.shape[0]
    vmem = pl.BlockSpec(memory_space=pltpu.VMEM)
    smem = pl.BlockSpec(memory_space=pltpu.SMEM)
    anywhere = pl.BlockSpec(memory_space=pl.ANY)
    shape = (n // 16, positions, 16, n) if direct else (positions, n, n)
    count = 2 * plan.keep

    def body(*refs):
        slice_body(plan, direct, *refs)

    return pl.pallas_call(
        body,
        out_shape=jax.ShapeDtypeStruct(shape, BF16),
        in_specs=[smem] + [anywhere] * 4 + [vmem] * 8,
        out_specs=vmem,
        scratch_shapes=[
            pltpu.VMEM((2,) + own.shape, BF16),
            pltpu.VMEM((G, G), F32),
            pltpu.VMEM((positions, 2, n, n), F32),
            pltpu.VMEM((positions, 2, n, n), BF16),
            pltpu.VMEM((positions, 2, count, n), F32),
            pltpu.VMEM((positions, 2 * count, n), BF16),
            pltpu.VMEM((positions, 2 * count, n), F32),
            pltpu.SemaphoreType.DMA((2, own.shape[0])),
            pltpu.SemaphoreType.DMA((2,)),
        ],
        name="multislice",
    )(
        offsets,
        own,
        got,
        *start,
        prop,
        jnp.asarray(plan.fwd_y, BF16),
        jnp.asarray(plan.fwd_x, BF16),
        jnp.asarray(plan.inv_y, BF16),
        jnp.asarray(plan.inv_x, BF16),
        jnp.asarray(plan.last_y, BF16),
        jnp.asarray(plan.last_x, BF16),
        jnp.asarray(plan.aperture_last),
    )


def scan_matrix(positions):
    index = np.arange(positions)
    angle = 2.0 * np.pi / positions * (np.outer(index, index) % positions)
    return np.concatenate([np.cos(angle), -np.sin(angle)]) / math.sqrt(positions)


def on_device(
    atom_positions,
    atom_species,
    atom_slice,
    species_amp,
    species_width,
    probe_spectrum,
    window_offsets,
    probe_shifts,
    slice_phase,
):
    devices = lax.axis_size("probe")
    n = probe_spectrum.shape[-1]
    layers = slice_phase.shape[0] + 1
    plan = Plan(n)
    species = species_amp.shape[0]
    atoms = sort_atoms(atom_positions, atom_species, atom_slice, layers, species)
    atoms = gather_atoms(atoms, devices)
    shifts = (probe_shifts + window_offsets) & (n - 1)
    half = -(-shifts.shape[0] // 4)
    start_a, prop = init(plan, shifts[:half], slice_phase, probe_spectrum)
    *atoms, start_a, prop = lax.optimization_barrier((*atoms, start_a, prop))
    own = build(plan, atoms, species_amp, species_width, layers)
    got = swap(own, 1, devices)
    shifts, own = lax.optimization_barrier((shifts[half:], own))
    start_b = init(plan, shifts, None, probe_spectrum)
    rows = n // devices
    direct = rows % 16 == 0
    intensity = multislice(plan, window_offsets, own, got, (start_a, start_b), prop, direct)
    positions = window_offsets.shape[0]
    if direct:
        received = lax.all_to_all(intensity, "probe", split_axis=0, concat_axis=0, tiled=True)
    else:
        pieces = intensity.reshape(positions, devices, rows, n)
        received = lax.all_to_all(pieces, "probe", split_axis=1, concat_axis=0, tiled=True)
    count = positions * devices
    received = received.reshape(count, rows * n)
    product = dot(jnp.asarray(scan_matrix(count), BF16), received)
    return product.reshape(2, count, rows * n)


def solution(mesh):
    placed = (
        P(None, ("groups", "probe")),
        P(("groups", "probe")),
        P(("groups", "probe")),
        P(),
        P(),
        P(),
        P(("groups", "probe"), None),
        P(("groups", "probe"), None),
        P(),
    )
    return jax.shard_map(
        on_device, mesh=mesh, in_specs=placed, out_specs=P(None, "groups", "probe"), check_vma=False
    )
```
